32 devices in a mesh: seq: 8 (over y, x, core), head: 4 (over z).
Axes of the slice: x: 2, y: 2, z: 4, core: 2. Of those that a mesh axis runs over, the one named last changes fastest.
Arguments:
- stream: bfloat16 [2048, 768], P('seq'), may hold values from -6 to 6
- seq_flags: int32 [2048], P('seq'), may hold values from 0 to 1, as said below
- norm_gain: float32 [2, 768], replicated, may hold values from 0.5 to 1.5
- in_zx: bfloat16 [2, 2, 768, 1536], P(None, None, None, 'head'), may hold values from -0.21875 to 0.21875
- in_bc: bfloat16 [2, 768, 256], replicated, may hold values from -0.21875 to 0.21875
- in_dt: bfloat16 [2, 768, 24], P(None, None, 'head'), may hold values from -0.109375 to 0.109375
- dt_bias: float32 [2, 24], P(None, 'head'), may hold values from -4 to -1
- a_log: float32 [2, 24], P(None, 'head'), may hold values from -7 to 1
- skip_d: float32 [2, 24], P(None, 'head'), may hold values from 0.5 to 1.5
- conv_x: float32 [2, 4, 1536], P(None, None, 'head'), may hold values from -3 to 3
- conv_x_bias: float32 [2, 1536], P(None, 'head'), may hold values from -0.5 to 0.5
- conv_bc: float32 [2, 4, 256], replicated, may hold values from -3 to 3
- conv_bc_bias: float32 [2, 256], replicated, may hold values from -0.5 to 0.5
- gate_gain: float32 [2, 1536], P(None, 'head'), may hold values from 0.5 to 1.5
- out_proj: bfloat16 [2, 1536, 768], P(None, 'head'), may hold values from -0.15625 to 0.15625
- cotangent: bfloat16 [2048, 768], P('seq'), may hold values from -6 to 6
Outputs:
- output: float32 [2048, 768], P('seq')
- grad_stream: float32 [2048, 768], P('seq')
- grad_norm_gain: float32 [2, 768], replicated
- grad_in_zx: float32 [2, 2, 768, 1536], P(None, None, None, 'head')
- grad_in_bc: float32 [2, 768, 256], replicated
- grad_in_dt: float32 [2, 768, 24], P(None, None, 'head')
- grad_dt_bias: float32 [2, 24], P(None, 'head')
- grad_a_log: float32 [2, 24], P(None, 'head')
- grad_skip_d: float32 [2, 24], P(None, 'head')
- grad_conv_x: float32 [2, 4, 1536], P(None, None, 'head')
- grad_conv_x_bias: float32 [2, 1536], P(None, 'head')
- grad_conv_bc: float32 [2, 4, 256], replicated
- grad_conv_bc_bias: float32 [2, 256], replicated
- grad_gate_gain: float32 [2, 1536], P(None, 'head')
- grad_out_proj: float32 [2, 1536, 768], P(None, 'head')
The draws below stay inside these ranges and needn't reach their ends.
Inputs may be any that keep to these rules, and one draw needn't show every extreme that they name: seq_flags is 1 at position 0, and every other 1 stands at a position that is a multiple of 8.
All inputs are finite; a program needn't handle non-finite values.
Results may differ from the reference program's by a relative error of at most 0.04.
Values may be sent and summed in bfloat16 or wider, within the bound.
No kernel may reach another device: no remote copies, remote signals or barrier semaphores. Data moves between devices by JAX's collectives and lax.ppermute only.
A program may use at most 128 MiB of HBM per device.

```python
import jax
import jax.numpy as jnp
from jax import lax

D = 768
H = 24
P_SIZE = 64
N = 128
CONV = 4
GROUP = 256
LAYERS = 2
TOK_DEV = 256
DI = 1536
TOKENS = 2048


def draw_seq_flags(key, part):
    picks = jax.random.randint(key, (TOKENS,), 0, TOK_DEV)
    places = jnp.arange(TOKENS, dtype=jnp.int32)
    marked = jnp.where((places % 8 == 0) & (picks == 0), 1, 0)
    marked = jnp.where(places == 0, 1, marked)
    return marked.astype(jnp.int32)


def shard_levels(stream_key, dims, cuts, low, high):
    factor_of = 1.0
    for position, blocks in cuts:
        heights = jax.random.uniform(jax.random.fold_in(jax.random.fold_in(stream_key, 6), position), (blocks,), jnp.float32, low / len(cuts), high / len(cuts))
        factor_of = factor_of * jnp.repeat(jnp.exp(heights), dims[position] // blocks).reshape((-1,) + (1,) * (len(dims) - 1 - position))
    return factor_of


def scatter_about(rng, dims, scale, bound, split=(), held_as=jnp.bfloat16):
    factor_of = shard_levels(rng, dims, split, -0.22, 0.18) if split else 1.0
    values = jax.random.normal(rng, dims, jnp.float32) * scale * factor_of
    return jnp.minimum(jnp.maximum(values, -bound), bound).astype(held_as)


def setup_inputs(seed: int = 0) -> dict:
    key_list = jax.random.split(jax.random.key(seed), 17)
    stream = scatter_about(key_list[0], (TOKENS, D), 1.0, 6.0, ((0, 8),))
    seq_flags = draw_seq_flags(jax.random.fold_in(key_list[16], 71), 0)
    norm_gain = jnp.clip(1.0 + 0.1 * jax.random.normal(key_list[2], (LAYERS, D), jnp.float32), 0.5, 1.5)
    in_zx = scatter_about(key_list[3], (LAYERS, 2, D, DI), D ** -0.5, 0.21875, ((3, 4),))
    in_bc = scatter_about(key_list[4], (LAYERS, D, 2 * N), D ** -0.5, 0.21875)
    in_dt = scatter_about(key_list[5], (LAYERS, D, H), (4 * D) ** -0.5, 0.109375, ((2, 4),))
    dt_bias = jnp.clip(-4.0 + 3.0 * jax.random.uniform(key_list[6], (LAYERS, H), jnp.float32) ** shard_levels(key_list[6], (LAYERS, H), ((1, 4),), -0.2, 0.2), -4.0, -1.0)
    a_log = jnp.clip(-7.0 + 8.0 * jax.random.uniform(key_list[7], (LAYERS, H), jnp.float32) ** shard_levels(key_list[7], (LAYERS, H), ((1, 4),), -0.2, 0.2), -7.0, 1.0)
    skip_d = jnp.clip(0.5 + 1.0 * jax.random.uniform(key_list[8], (LAYERS, H), jnp.float32) ** shard_levels(key_list[8], (LAYERS, H), ((1, 4),), -0.2, 0.2), 0.5, 1.5)
    conv_x = scatter_about(key_list[9], (LAYERS, CONV, DI), CONV ** -0.5, 3.0, ((2, 4),), jnp.float32)
    conv_x_bias = jnp.clip(jax.random.uniform(key_list[10], (LAYERS, DI), jnp.float32, -0.5, 0.5) * shard_levels(key_list[10], (LAYERS, DI), ((1, 4),), -0.4, 0.0), -0.5, 0.5)
    conv_bc = scatter_about(key_list[11], (LAYERS, CONV, 2 * N), CONV ** -0.5, 3.0, (), jnp.float32)
    conv_bc_bias = jnp.clip(jax.random.uniform(key_list[12], (LAYERS, 2 * N), jnp.float32, -0.5, 0.5), -0.5, 0.5)
    gate_gain = jnp.clip(1.0 + 0.1 * jax.random.normal(key_list[13], (LAYERS, DI), jnp.float32), 0.5, 1.5)
    out_proj = scatter_about(key_list[14], (LAYERS, DI, D), DI ** -0.5, 0.15625, ((1, 4),))
    cotangent = scatter_about(key_list[15], (TOKENS, D), 1.0, 6.0, ((0, 8),))
    return dict(stream=stream, seq_flags=seq_flags, norm_gain=norm_gain, in_zx=in_zx, in_bc=in_bc, in_dt=in_dt, dt_bias=dt_bias, a_log=a_log, skip_d=skip_d, conv_x=conv_x, conv_x_bias=conv_x_bias, conv_bc=conv_bc, conv_bc_bias=conv_bc_bias, gate_gain=gate_gain, out_proj=out_proj, cotangent=cotangent)


EPS = 1e-05
PRECISE = lax.Precision.HIGHEST

def contract_rows(left, right):
    return lax.dot_general(left, right, (((0,), (0,)), ((), ())), preferred_element_type=jnp.float32)

def outer_t(left, right):
    return lax.dot_general(left, right, (((1,), (1,)), ((), ())), preferred_element_type=jnp.float32)

def norm_rows(residual, gain_row):
    inv_rms = lax.rsqrt(lax.optimization_barrier(jnp.mean(residual * residual, axis=1, keepdims=True)) + EPS)
    return residual * inv_rms * gain_row[None, :]

def conv_causal(extended, weights, conv_bias, starts_ext):
    conv_taps = weights.shape[0]
    length = extended.shape[0] - conv_taps + 1
    running = jnp.cumsum(starts_ext)
    result = jnp.zeros((length, extended.shape[1]), extended.dtype) + conv_bias[None, :]
    for offset in range(conv_taps):
        first_row = conv_taps - 1 - offset
        source = extended[first_row:first_row + length]
        counts = running[conv_taps - 1:conv_taps - 1 + length] - running[first_row:first_row + length]
        validity = jnp.where(counts == 0, 1.0, 0.0).astype(extended.dtype)
        result = result + weights[first_row][None, :] * source * validity[:, None]
    return result

def ssd_group(carry_state, values, keys_in, queries, step_sizes, rates, starts):
    decay_log = step_sizes * rates[None, :]
    cumulative = jnp.cumsum(decay_log, axis=0)
    segment = jnp.cumsum(starts)
    length = starts.shape[0]
    rows_idx = lax.broadcasted_iota(jnp.int32, (length, length), 0)
    cols_idx = lax.broadcasted_iota(jnp.int32, (length, length), 1)
    allowed = (rows_idx >= cols_idx) & (segment[:, None] == segment[None, :])
    spread = cumulative.T[:, :, None] - cumulative.T[:, None, :]
    decay_mat = jnp.where(allowed[None], jnp.exp(jnp.where(allowed[None], spread, 0.0)), 0.0)
    scores = jnp.dot(queries, keys_in.T, precision=PRECISE)
    mixing = decay_mat * scores[None] * step_sizes.T[:, None, :]
    inside = jnp.einsum('hts,shp->thp', mixing, values, precision=PRECISE)
    opening = jnp.exp(cumulative) * jnp.where(segment == 0, 1.0, 0.0)[:, None]
    carried = jnp.einsum('tn,hnp->thp', queries, carry_state, precision=PRECISE) * opening[:, :, None]
    closing = jnp.exp(cumulative[-1][None, :] - cumulative) * jnp.where(segment == segment[-1], 1.0, 0.0)[:, None] * step_sizes
    kept_share = jnp.exp(cumulative[-1]) * jnp.where(segment[-1] == 0, 1.0, 0.0)
    new_state = carry_state * kept_share[:, None, None] + jnp.einsum('sn,shp->hnp', keys_in, values * closing[:, :, None], precision=PRECISE)
    return (inside + carried, new_state)

def ssd_all(values, keys_in, queries, step_sizes, rates, starts):
    token_total = starts.shape[0]
    block_count = token_total // GROUP
    pieces = (values.reshape(block_count, GROUP, H, P_SIZE), keys_in.reshape(block_count, GROUP, N), queries.reshape(block_count, GROUP, N), step_sizes.reshape(block_count, GROUP, H), starts.reshape(block_count, GROUP))

    def advance(carry_state, window):
        result, new_state = ssd_group(carry_state, window[0], window[1], window[2], window[3], rates, window[4])
        return (new_state, result)
    _, block_outs = lax.scan(advance, jnp.zeros((H, N, P_SIZE), values.dtype), pieces)
    return block_outs.reshape(token_total, H, P_SIZE)

def mixer_core(activated, gate_in, dt_raw, dt_bias, a_log, skip_d, gate_gain, starts):
    values = activated[:, :DI].reshape(-1, H, P_SIZE)
    keys_in = activated[:, DI:DI + N]
    queries = activated[:, DI + N:]
    step_sizes = jax.nn.softplus(dt_raw + dt_bias[None, :])
    rates = -jnp.exp(a_log)
    mixed_out = ssd_all(values, keys_in, queries, step_sizes, rates, starts)
    mixed_out = mixed_out + skip_d[None, :, None] * values
    gated_out = mixed_out.reshape(-1, DI) * jax.nn.silu(gate_in)
    inv_rms = lax.rsqrt(lax.optimization_barrier(jnp.mean(gated_out * gated_out, axis=1, keepdims=True)) + EPS)
    return gated_out * inv_rms * gate_gain[None, :]

def layer_forward(residual, starts, params):
    norm_gain, in_zx, in_bc, in_dt, dt_bias, a_log, skip_d, conv_x, conv_x_bias, conv_bc, conv_bc_bias, gate_gain, out_proj = params
    normed = norm_rows(residual, norm_gain).astype(jnp.bfloat16)
    gate_in = jnp.dot(normed, in_zx[0], preferred_element_type=jnp.float32)
    before = jnp.concatenate([jnp.dot(normed, in_zx[1], preferred_element_type=jnp.float32).astype(jnp.bfloat16), jnp.dot(normed, in_bc, preferred_element_type=jnp.float32).astype(jnp.bfloat16)], axis=1)
    dt_raw = jnp.dot(normed, in_dt, preferred_element_type=jnp.float32)
    conv_taps = conv_x.shape[0]
    channels = before.shape[1]
    extended = jnp.concatenate([jnp.zeros((conv_taps - 1, channels), jnp.float32), before.astype(jnp.float32)], axis=0)
    starts_ext = jnp.concatenate([jnp.zeros((conv_taps - 1,), jnp.float32), starts])
    weights = jnp.concatenate([conv_x, conv_bc], axis=1)
    conv_bias = jnp.concatenate([conv_x_bias, conv_bc_bias])
    activated = jax.nn.silu(conv_causal(extended, weights, conv_bias, starts_ext)).astype(jnp.bfloat16)
    core = mixer_core(activated.astype(jnp.float32), gate_in, dt_raw, dt_bias, a_log, skip_d, gate_gain, starts)
    outgoing = core.astype(jnp.bfloat16)
    next_stream = residual + jnp.dot(outgoing, out_proj, preferred_element_type=jnp.float32)
    stored = (normed, gate_in, dt_raw, extended, starts_ext, weights, conv_bias, activated, outgoing)
    return (next_stream, stored)

def layer_backward(residual, starts, params, stored, grad_next):
    norm_gain, in_zx, in_bc, in_dt, dt_bias, a_log, skip_d, conv_x, conv_x_bias, conv_bc, conv_bc_bias, gate_gain, out_proj = params
    normed, gate_in, dt_raw, extended, starts_ext, weights, conv_bias, activated, outgoing = stored
    conv_taps = conv_x.shape[0]
    low_grad = grad_next.astype(jnp.bfloat16)
    grad_out_proj = contract_rows(outgoing, low_grad)
    grad_outgoing = outer_t(low_grad, out_proj)

    def core_fn(act_in, gate_val, raw_val, bias_val, alog_val, skip_val, gain_val):
        return mixer_core(act_in, gate_val, raw_val, bias_val, alog_val, skip_val, gain_val, starts)
    _, pull_core = jax.vjp(core_fn, activated.astype(jnp.float32), gate_in, dt_raw, dt_bias, a_log, skip_d, gate_gain)
    g_act, g_gate, g_raw, g_dt_bias, g_a_log, g_skip, g_gate_gain = pull_core(grad_outgoing)

    def conv_fn(ext_val, wts_val, bias_val):
        return jax.nn.silu(conv_causal(ext_val, wts_val, bias_val, starts_ext))
    _, pull_conv = jax.vjp(conv_fn, extended, weights, conv_bias)
    g_ext, g_weights, g_bias = pull_conv(g_act)
    g_before = g_ext[conv_taps - 1:]
    low_gate = g_gate.astype(jnp.bfloat16)
    low_conv = g_before.astype(jnp.bfloat16)
    low_raw = g_raw.astype(jnp.bfloat16)
    grad_in_zx = jnp.stack([contract_rows(normed, low_gate), contract_rows(normed, low_conv[:, :DI])])
    grad_in_bc = contract_rows(normed, low_conv[:, DI:])
    grad_in_dt = contract_rows(normed, low_raw)
    g_normed = outer_t(low_gate, in_zx[0]) + outer_t(low_conv[:, :DI], in_zx[1]) + outer_t(low_conv[:, DI:], in_bc) + outer_t(low_raw, in_dt)
    _, pull_norm = jax.vjp(norm_rows, residual, norm_gain)
    g_resid, g_norm_gain = pull_norm(g_normed)
    weight_grads = (g_norm_gain, grad_in_zx, grad_in_bc, grad_in_dt, g_dt_bias, g_a_log, g_skip, g_weights[:, :DI], g_bias[:DI], g_weights[:, DI:], g_bias[DI:], g_gate_gain, grad_out_proj)
    return (grad_next + g_resid, weight_grads)

def reference(stream, seq_flags, norm_gain, in_zx, in_bc, in_dt, dt_bias, a_log, skip_d, conv_x, conv_x_bias, conv_bc, conv_bc_bias, gate_gain, out_proj, cotangent):
    starts = seq_flags.astype(jnp.float32)
    params_all = (norm_gain, in_zx, in_bc, in_dt, dt_bias, a_log, skip_d, conv_x, conv_x_bias, conv_bc, conv_bc_bias, gate_gain, out_proj)
    residual = stream.astype(jnp.float32)
    inputs_kept = []
    stores = []
    for depth in range(LAYERS):
        params = tuple((member[depth] for member in params_all))
        inputs_kept.append(residual)
        residual, stored = layer_forward(residual, starts, params)
        stores.append(stored)
    output = residual
    gradient = cotangent.astype(jnp.float32)
    per_layer = [None] * LAYERS
    for depth in reversed(range(LAYERS)):
        params = tuple((member[depth] for member in params_all))
        gradient, weight_grads = layer_backward(inputs_kept[depth], starts, params, stores[depth], gradient)
        per_layer[depth] = weight_grads
    stacked = [jnp.stack([per_layer[depth][number] for depth in range(LAYERS)]) for number in range(13)]
    return (output, gradient, stacked[0], stacked[1], stacked[2], stacked[3], stacked[4], stacked[5], stacked[6], stacked[7], stacked[8], stacked[9], stacked[10], stacked[11], stacked[12])
```

```python
import functools

import jax
import jax.numpy as jnp
from jax import lax
from jax.experimental import pallas as pl
from jax.experimental.pallas import tpu as pltpu
from jax.sharding import PartitionSpec as P

P_SIZE = 64
N = 128
LAYERS = 2
EPS = 1e-05
LANES = 128
HALO = 8
TH = 16
F32 = jnp.float32
BF = jnp.bfloat16
HI = lax.Precision.HIGHEST


def dot(a, b, dims=((1,), (0,)), precision=None):
    return lax.dot_general(a, b, (dims, ((), ())), preferred_element_type=F32, precision=precision)


NT = ((1,), (1,))
TN = ((0,), (0,))


def iotas(rows, cols):
    return (
        lax.broadcasted_iota(jnp.int32, (rows, cols), 0),
        lax.broadcasted_iota(jnp.int32, (rows, cols), 1),
    )


def tri(rows, lower=True):
    r, c = iotas(rows, rows)
    return jnp.where(c <= r if lower else c >= r, 1.0, 0.0)


def flags8(flags_ref):
    return jnp.broadcast_to(flags_ref[...].astype(F32), (8, flags_ref.shape[1])).astype(BF)


def seg_col(flags_ref):
    t = flags_ref.shape[1]
    return dot(tri(t).astype(BF), flags8(flags_ref), NT)[:, 0:1]


def seg_row(flags_ref):
    t = flags_ref.shape[1]
    return dot(flags8(flags_ref), tri(t, False).astype(BF))[0:1, :]


def windows(flags_ref, taps):
    t = flags_ref.shape[1]
    r, c = iotas(t, t)
    fl = flags8(flags_ref)
    out = [None]
    for d in range(1, taps):
        band = jnp.where((c <= r) & (c > r - d), 1.0, 0.0).astype(BF)
        out.append(jnp.where(dot(band, fl, NT)[:, 0:1] == 0.0, 1.0, 0.0))
    return out


def spread(cols, heads):
    rows = cols.shape[0]
    return jnp.concatenate(
        [jnp.broadcast_to(cols[:, h : h + 1], (rows, P_SIZE)) for h in range(heads)], axis=1
    )


def head_sum(z):
    r, c = iotas(z.shape[1], LANES)
    lo = c * P_SIZE
    pick = jnp.where((r >= lo) & (r < lo + P_SIZE), 1.0, 0.0)
    return dot(z, pick, precision=HI)


def sigmoid(v):
    return 1.0 / (1.0 + jnp.exp(-v))


def softplus(v):
    return jnp.maximum(v, 0.0) + jnp.log(1.0 + jnp.exp(-jnp.abs(v)))


def two(col, width):
    rows = col.shape[0]
    _, c = iotas(rows, width)
    high = col.astype(BF).astype(F32)
    low = col - high
    return jnp.where(c == 0, high, jnp.where(c == 1, low, 0.0)).astype(BF)


def untwo(block):
    b = block.astype(F32)
    return b[:, 0:1] + b[:, 1:2]


def through_rows(row):
    r, _ = iotas(TH, row.shape[1])
    high = row.astype(BF).astype(F32)
    return jnp.where(r == 0, high, jnp.where(r == 1, row - high, 0.0)).astype(BF)


def closing_parts(cum, segc):
    t = cum.shape[0]
    last, seg_last = cum[t - 1 : t, :], segc[t - 1 : t, :]
    closing = jnp.exp(last - cum) * jnp.where(segc == seg_last, 1.0, 0.0)
    through = jnp.exp(last) * jnp.where(seg_last == 0.0, 1.0, 0.0)
    return closing, through


def norm_of(r, gain):
    inv = lax.rsqrt(jnp.mean(r * r, axis=1, keepdims=True) + EPS)
    return r * inv * gain


def at_rows(s_ref, k, rows):
    return pl.ds(pl.multiple_of(s_ref[k] * rows, rows), rows)


def k_project(layer, nh, refs):
    if layer == 0:
        stream, gain, wz, wx, wbc, wdt, gate, cin, dtr, normed = refs
        nm = norm_of(stream[...].astype(F32), gain[0:1, :]).astype(BF)
        normed[...] = nm
    else:
        s_ref, chunks, refs = refs[0], refs[1 : 1 + nh], refs[1 + nh :]
        wz, wx, wbc, wdt, gate, cin, dtr, normed, invc = refs
        rows, d = chunks[0].shape[0], normed.shape[1]
        for k in range(nh):
            normed[at_rows(s_ref, k, rows), :] = chunks[k][:, :d]
            both = jnp.broadcast_to(untwo(chunks[k][:, d:]), (rows, LANES))
            invc[at_rows(s_ref, k, rows), :] = both
        nm = normed[...]
    ch = wz.shape[1]
    gate[...] = dot(nm, wz[...])
    cin[:, :ch] = dot(nm, wx[...]).astype(BF)
    cin[:, ch:] = dot(nm, wbc[...]).astype(BF)
    dtr[...] = dot(nm, wdt[...])


def k_conv(layer, heads, raw_halo, refs):
    (halo, gain, cin, dtr, flags, wx, wbc, cx, cxb, cbc, cbcb, dtb, alog,
     act, ds, hc, step, cum, pay, ext) = refs
    t, cc = cin.shape
    ch = wx.shape[1]
    taps = cx.shape[1]
    hn = halo[...]
    if raw_halo:
        hn = norm_of(hn.astype(F32), gain[layer : layer + 1, :]).astype(BF)
    hx, hb = dot(hn, wx[...]).astype(BF), dot(hn, wbc[...]).astype(BF)
    hc[:, :ch] = hx
    hc[:, ch:] = hb
    ext[:HALO, :ch] = hx.astype(F32)
    ext[:HALO, ch:] = hb.astype(F32)
    ext[HALO:, :] = cin[...].astype(F32)
    valid = windows(flags, taps)
    for lo, hi, w, b in ((0, ch, cx, cxb), (ch, cc, cbc, cbcb)):
        v = b[layer : layer + 1, :] + w[layer, taps - 1 : taps, :] * ext[HALO:, lo:hi]
        for d in range(1, taps):
            tap = w[layer, taps - 1 - d : taps - d, :]
            v = v + tap * (ext[HALO - d : HALO - d + t, lo:hi] * valid[d])
        sig = sigmoid(v)
        act[:, lo:hi] = (v * sig).astype(BF)
        ds[:, lo:hi] = (sig * (1.0 + v * (1.0 - sig))).astype(BF)
    st = softplus(dtr[...] + dtb[layer : layer + 1, :])
    rate = -jnp.exp(alog[layer : layer + 1, :])
    cm = dot(tri(t), st * rate, precision=HI)
    step[...] = st
    cum[...] = cm
    closing, through = closing_parts(cm, seg_col(flags))
    x = act[:, :ch].astype(F32)
    xs = (x * spread(st * closing, heads)).astype(BF)
    pay[:N, :] = dot(act[:, ch : ch + N], xs, TN).astype(BF)
    pay[N:, :] = through_rows(spread(through, heads))


def k_combine(first, last, refs):
    flag, own, got = refs[0], refs[1], refs[2]
    refs = refs[3:]
    if not first:
        pre, q = refs[0], refs[1]
        refs = refs[2:]
    mine = flag[0] == 1
    s_own, s_got = own[:N, :].astype(F32), got[:N, :].astype(F32)
    t_own = own[N : N + 1, :].astype(F32) + own[N + 1 : N + 2, :].astype(F32)
    t_got = got[N : N + 1, :].astype(F32) + got[N + 1 : N + 2, :].astype(F32)
    if first:
        new_pre = jnp.where(mine, s_got, 0.0)
        new_q = jnp.where(mine, t_got, 1.0)
    else:
        qv = q[0:1, :]
        new_pre = pre[...] + jnp.where(mine, qv * s_got, 0.0)
        new_q = qv * jnp.where(mine, t_got, 1.0)
    refs[0][...] = new_pre.astype(refs[0].dtype)
    if not last:
        refs[1][...] = jnp.broadcast_to(new_q, (8, new_q.shape[1]))
        total = refs[2]
        total[:N, :] = (
            jnp.where(mine, s_own, s_got)
            + jnp.where(mine, t_own, t_got) * jnp.where(mine, s_got, s_own)
        ).astype(BF)
        total[N:, :] = through_rows(t_own * t_got)


def decay_of(cum_col, cum_row, allowed):
    return jnp.exp(jnp.where(allowed, cum_col - cum_row, -1e30))


def k_inside(heads, refs):
    act, step, cum, flags, yin = refs
    t = act.shape[0]
    ch = yin.shape[1]
    r, c = iotas(t, t)
    allowed = (c <= r) & (seg_col(flags) == seg_row(flags))
    scores = dot(act[:, ch + N :], act[:, ch : ch + N], NT)
    cm = cum[...]
    cmt = cm.T
    xs = (act[:, :ch].astype(F32) * spread(step[...], heads)).astype(BF)
    for h in range(heads):
        m = decay_of(cm[:, h : h + 1], cmt[h : h + 1, :], allowed) * scores
        cols = slice(h * P_SIZE, (h + 1) * P_SIZE)
        yin[:, cols] = dot(m.astype(BF), xs[:, cols])


def k_output(layer, heads, nh, refs):
    s_ref, pre, act, cum, flags, yin, gate, gain, skip, wo = refs[:10]
    refs = refs[10:]
    final = layer == LAYERS - 1
    if final:
        low = refs[0]
        refs = refs[1:]
    y0, refs = refs[0], refs[1:]
    chunks, refs = refs[:nh], refs[nh:]
    ch = yin.shape[1]
    d = wo.shape[1]
    opening = jnp.exp(cum[...]) * jnp.where(seg_col(flags) == 0.0, 1.0, 0.0)
    y = yin[...] + dot(act[:, ch + N :], pre[...]) * spread(opening, heads)
    y0[...] = y
    mixed = y + spread(skip[layer : layer + 1, :], heads) * act[:, :ch].astype(F32)
    gi = gate[...]
    gated = mixed * (gi * sigmoid(gi))
    sq = jnp.sum(gated * gated, axis=1, keepdims=True)
    scaled = gated * gain[layer : layer + 1, :]
    scratch = refs[-1]
    scratch[:, :d] = dot(scaled.astype(BF), wo[...]).astype(BF)
    scratch[:, d:] = two(sq, LANES)
    rows = chunks[0].shape[0]
    for k in range(nh):
        chunks[k][...] = scratch[at_rows(s_ref, k, rows), :]
    if final:
        gout, small = refs[0], refs[1]
        go = dot(low[...], wo[...], NT)
        gout[...] = go
        cross = jnp.sum(go * scaled, axis=1, keepdims=True)
        t = sq.shape[0]
        _, c = iotas(t, LANES)
        cols = jnp.where(c == 0, sq, jnp.where(c == 1, cross, 0.0))
        small[...] = cols.T[:8, :]


def k_stream(layer, nh, refs):
    s_ref, parts, refs = refs[0], refs[1 : 1 + nh], refs[1 + nh :]
    own, gain, width, r_out, tot_out, pay = refs[:3] + refs[3:]
    rows, wide = parts[0].shape
    d = wide - LANES
    total = parts[0][:, :d].astype(F32)
    sq = untwo(parts[0][:, d:])
    for p in parts[1:]:
        total = total + p[:, :d].astype(F32)
        sq = sq + untwo(p[:, d:])
    inv = lax.rsqrt(sq * width[0] + EPS)
    r = own[at_rows(s_ref, 0, rows), :].astype(F32) + total * inv
    r_out[...] = r
    tot_out[...] = total
    pay[:, :d] = norm_of(r, gain[layer + 1 : layer + 2, :]).astype(BF)
    pay[:, d:] = two(inv, LANES)


def k_stream_last(nh, refs):
    s_ref, parts, refs = refs[0], refs[1 : 1 + nh], refs[1 + nh :]
    own, width, r_out = refs
    rows, wide = parts[0].shape
    d = wide - LANES
    total = parts[0][:, :d].astype(F32)
    sq = untwo(parts[0][:, d:])
    for p in parts[1:]:
        total = total + p[:, :d].astype(F32)
        sq = sq + untwo(p[:, d:])
    r_out[...] = (own[...] + total * lax.rsqrt(sq * width[0] + EPS)).astype(BF)


def k_join(nh, refs):
    s_ref, parts, out = refs[0], refs[1 : 1 + nh], refs[1 + nh]
    rows = parts[0].shape[0]
    for k in range(nh):
        out[at_rows(s_ref, k, rows), :] = parts[k][...].astype(F32)


def k_gate_back(layer, heads, nh, refs):
    final = layer == LAYERS - 1
    if final:
        smalls, refs = refs[:nh], refs[nh:]
        gout, width, gain, y0, gate, act, cum, flags, skip = refs[:9]
        refs = refs[9:]
        acc = smalls[0][...]
        for s in smalls[1:]:
            acc = acc + s[...]
        t = acc.shape[1]
        cols = jnp.concatenate([acc, jnp.zeros((LANES - 8, t), F32)], axis=0).T
        inv = lax.rsqrt(cols[:, 0:1] * width[0] + EPS)
        cross = cols[:, 1:2]
        go = gout[...]
        pay, gm, lowgate, og, small = refs
    else:
        s_ref, chunks, refs = refs[0], refs[1 : 1 + nh], refs[1 + nh :]
        wo, invc, width, gain, y0, gate, act, cum, flags, skip = refs[:10]
        pay, gm, lowgate, og, small, low, crs = refs[10:]
        rows, d = chunks[0].shape[0], wo.shape[1]
        for k in range(nh):
            low[at_rows(s_ref, k, rows), :] = chunks[k][:, :d]
            both = jnp.broadcast_to(untwo(chunks[k][:, d:]), (rows, LANES))
            crs[at_rows(s_ref, k, rows), :] = both
        cross = crs[:, 0:1]
        inv = invc[:, 0:1]
        go = dot(low[...], wo[...], NT)
    ch = y0.shape[1]
    gn = gain[layer : layer + 1, :]
    x = act[:, :ch].astype(F32)
    mixed = y0[...] + spread(skip[layer : layer + 1, :], heads) * x
    gi = gate[...]
    sig = sigmoid(gi)
    silu = gi * sig
    gated = mixed * silu
    ginv = gated * inv
    og[...] = (ginv * gn).astype(BF)
    g_gated = inv * (gn * go) - ginv * (inv * inv * cross * width[0])
    g_mixed = g_gated * silu
    lowgate[...] = (g_gated * mixed * (sig * (1.0 + gi * (1.0 - sig)))).astype(BF)
    gm[...] = g_mixed.astype(BF)
    segc = seg_col(flags)
    cm = cum[...]
    opening = jnp.exp(cm) * jnp.where(segc == 0.0, 1.0, 0.0)
    _, through = closing_parts(cm, segc)
    grad = dot(act[:, ch + N :], (g_mixed * spread(opening, heads)).astype(BF), TN)
    pay[:N, :] = grad.astype(BF)
    pay[N:, :] = through_rows(spread(through, heads))
    r, _ = iotas(8, ch)
    row0 = jnp.sum(go * ginv, axis=0, keepdims=True)
    row1 = jnp.sum(g_mixed * x, axis=0, keepdims=True)
    small[...] = jnp.where(r == 0, row0, jnp.where(r == 1, row1, 0.0))


def k_inside_back(heads, refs):
    (act, step, cum, flags, gm, pre, low, og, normed, lowgate,
     dxs, dbc, wout, wz) = refs
    t, ch = gm.shape
    r, c = iotas(t, t)
    segc = seg_col(flags)
    allowed = (c <= r) & (segc == seg_row(flags))
    keys, queries = act[:, ch : ch + N], act[:, ch + N :]
    scores = dot(queries, keys, NT)
    cm = cum[...]
    cmt = cm.T
    xs = (act[:, :ch].astype(F32) * spread(step[...], heads)).astype(BF)
    dy = gm[...]
    acc = jnp.zeros((t, t), F32)
    for h in range(heads):
        cols = slice(h * P_SIZE, (h + 1) * P_SIZE)
        decay = decay_of(cm[:, h : h + 1], cmt[h : h + 1, :], allowed)
        m = (decay * scores).astype(BF)
        dxs[:, cols] = dot(m, dy[:, cols], TN)
        acc = acc + dot(dy[:, cols], xs[:, cols], NT) * decay
    low_s = acc.astype(BF)
    dbc[:, :N] = dot(low_s, queries, TN)
    opening = jnp.exp(cm) * jnp.where(segc == 0.0, 1.0, 0.0)
    carried = (dy.astype(F32) * spread(opening, heads)).astype(BF)
    dbc[:, N:] = dot(low_s, keys) + dot(carried, pre[...], NT)
    wout[...] = dot(og[...], low[...], TN).astype(BF)
    wz[...] = dot(normed[...], lowgate[...], TN).astype(BF)


def k_state_back(layer, heads, refs):
    (g, pre, act, step, cum, dtr, flags, gm, y0, dxs, dbc, ds, cin, hc, cx, cbc, skip, dtb, alog,
     gb, gh, lowraw, small, ext, u_ref) = refs
    t, ch = gm.shape
    cc = cin.shape[1]
    taps = cx.shape[1]
    segc = seg_col(flags)
    cm = cum[...]
    st = step[...]
    closing, through = closing_parts(cm, segc)
    x = act[:, :ch].astype(F32)
    st_ch = spread(st, heads)
    clo_ch = spread(closing, heads)
    xs = (x * st_ch).astype(BF)
    xsf = xs.astype(F32)
    gst = g[...]
    gb16 = gst.astype(BF)
    keys = act[:, ch : ch + N]
    dwc = dot(keys, gb16) * clo_ch
    dkeys = dbc[:, :N] + dot((xsf * clo_ch).astype(BF), gb16, NT)
    dx_all = dxs[...] + dwc
    gmf = gm[...].astype(F32)
    z = head_sum(x * dx_all)
    dcum = head_sum(gmf * y0[...] - xsf * dx_all)
    at_last = jnp.sum(head_sum(xsf * dwc), axis=0, keepdims=True)
    keep = jnp.sum(gst * pre[...].astype(F32), axis=0, keepdims=True)
    at_last = at_last + through * head_sum(jnp.broadcast_to(keep, (8, ch)))[0:1, :]
    ddecay = dot(tri(t, False), dcum, precision=HI) + at_last
    rate = -jnp.exp(alog[layer : layer + 1, :])
    graw = (z + ddecay * rate) * sigmoid(dtr[...] + dtb[layer : layer + 1, :])
    lowraw[...] = graw.astype(BF)
    g_alog = jnp.sum(ddecay * st, axis=0, keepdims=True) * rate
    g_dtb = jnp.sum(graw, axis=0, keepdims=True)
    ext[:HALO, :] = hc[...].astype(F32)
    ext[HALO:, :] = cin[...].astype(F32)
    gv_x = (dx_all * st_ch + spread(skip[layer : layer + 1, :], heads) * gmf)
    valid = windows(flags, taps)
    for lo, hi, w, val in (
        (0, ch, cx, gv_x),
        (ch, ch + N, cbc, dkeys),
        (ch + N, cc, cbc, dbc[:, N:]),
    ):
        wl = lo if lo < ch else lo - ch
        gv = val * ds[:, lo:hi].astype(F32)
        small[4:5, lo:hi] = jnp.sum(gv, axis=0, keepdims=True)
        total = None
        for d in range(taps):
            u = gv if d == 0 else gv * valid[d]
            k = taps - 1 - d
            small[k : k + 1, lo:hi] = jnp.sum(
                u * ext[HALO - d : HALO - d + t, lo:hi], axis=0, keepdims=True
            )
            u_ref[0:HALO, lo:hi] = jnp.zeros((HALO, hi - lo), F32)
            u_ref[HALO : HALO + t, lo:hi] = u
            u_ref[HALO + t :, lo:hi] = jnp.zeros((HALO, hi - lo), F32)
            term = w[layer, k : k + 1, wl : wl + hi - lo] * u_ref[d : d + t + HALO, lo:hi]
            total = term if total is None else total + term
        gh[:, lo:hi] = total[:HALO, :]
        gb[:, lo:hi] = total[HALO:, :]
    small[5:8, :] = jnp.zeros((3, cc), F32)
    small[5:6, :LANES] = g_dtb
    small[6:7, :LANES] = g_alog


def k_back_project(refs):
    lowgate, gb, lowraw, wz, wx, wbc, wdt, part = refs
    ch = wz.shape[1]
    part[...] = (
        dot(lowgate[...], wz[...], NT)
        + dot(gb[:, :ch].astype(BF), wx[...], NT)
        + dot(gb[:, ch:].astype(BF), wbc[...], NT)
        + dot(lowraw[...], wdt[...], NT)
    )


def k_back_fix(nh, refs):
    s_ref, part, ret, wx, wbc = refs[:5]
    chunks, scratch = refs[5 : 5 + nh], refs[5 + nh]
    t = part.shape[0]
    ch = wx.shape[1]
    scratch[...] = part[...].astype(BF)
    low = ret[...].astype(BF)
    fix = dot(low[:, :ch], wx[...], NT) + dot(low[:, ch:], wbc[...], NT)
    fix = jnp.concatenate([jnp.zeros_like(fix), fix], axis=0)
    scratch[t - 2 * HALO :, :] = (part[t - 2 * HALO :, :] + fix).astype(BF)
    rows = chunks[0].shape[0]
    for k in range(nh):
        chunks[k][...] = scratch[at_rows(s_ref, k, rows), :]


def k_weights(refs):
    normed, gb, ret, lowraw, wx, wbc, wdt, scratch = refs
    t = gb.shape[0]
    ch = wx.shape[1]
    scratch[...] = gb[...].astype(BF)
    tail = gb[t - 2 * HALO :, :]
    fix = jnp.concatenate([jnp.zeros_like(ret[...]), ret[...]], axis=0)
    scratch[t - 2 * HALO :, :] = (tail + fix).astype(BF)
    nm = normed[...]
    wx[...] = dot(nm, scratch[:, :ch], TN).astype(BF)
    wbc[...] = dot(nm, scratch[:, ch:], TN).astype(BF)
    wdt[...] = dot(nm, lowraw[...], TN).astype(BF)


def k_norm_back(layer, nh, refs):
    s_ref, parts, refs = refs[0], refs[1 : 1 + nh], refs[1 + nh :]
    final = layer == LAYERS - 1
    if layer > 0:
        r_own, g_in, gain, total, g_out, gng, pay = refs
    else:
        r_own, g_in, gain, gng, pay = refs
    rows, d = parts[0].shape
    gn = parts[0][...].astype(F32)
    for p in parts[1:]:
        gn = gn + p[...].astype(F32)
    r = r_own[...] if layer > 0 else r_own[at_rows(s_ref, 0, rows), :].astype(F32)
    old = g_in[at_rows(s_ref, 0, rows), :].astype(F32) if final else g_in[...]
    inv = lax.rsqrt(jnp.mean(r * r, axis=1, keepdims=True) + EPS)
    ri = r * inv
    gg = gn * gain[layer : layer + 1, :]
    new = old + inv * (gg - ri * jnp.mean(gg * ri, axis=1, keepdims=True))
    gng[...] = jnp.broadcast_to(jnp.sum(gn * ri, axis=0, keepdims=True), (8, d))
    if layer > 0:
        g_out[...] = new
        low = new.astype(BF)
        pay[:, :d] = low
        cross = jnp.sum(low.astype(F32) * total[...], axis=1, keepdims=True)
        pay[:, d:] = two(cross, LANES)
    else:
        pay[...] = new.astype(BF)


SMEM = pl.BlockSpec(memory_space=pltpu.SMEM)


class Layered:
    def __init__(self, array, *lead):
        self.array, self.lead = array, lead


def call(body, name, args, outs, scratch=(), flops=0):
    specs, arrays = [], []
    size = 0
    for a in args:
        if isinstance(a, Layered):
            rest = a.array.shape[len(a.lead) :]
            lead = a.lead
            specs.append(
                pl.BlockSpec(
                    (None,) * len(lead) + rest,
                    functools.partial(lambda lead, n, i: lead + (0,) * n, lead, len(rest)),
                )
            )
            arrays.append(a.array)
            count = 1
            for s in rest:
                count *= s
            size += count * a.array.dtype.itemsize
        elif a.dtype == jnp.int32 and a.ndim == 1 or a.ndim == 1:
            specs.append(SMEM)
            arrays.append(a)
        else:
            specs.append(pl.BlockSpec(a.shape, functools.partial(lambda n, i: (0,) * n, a.ndim)))
            arrays.append(a)
            size += a.size * a.dtype.itemsize
    for s, t in outs:
        count = 1
        for k in s:
            count *= k
        size += count * jnp.dtype(t).itemsize

    def kernel(*refs):
        body(refs)

    return pl.pallas_call(
        kernel,
        out_shape=[jax.ShapeDtypeStruct(s, t) for s, t in outs],
        grid=(1,),
        in_specs=specs,
        out_specs=[
            pl.BlockSpec(s, functools.partial(lambda n, i: (0,) * n, len(s))) for s, _ in outs
        ],
        scratch_shapes=[pltpu.VMEM(s, t) for s, t in scratch],
        compiler_params=pltpu.CompilerParams(vmem_limit_bytes=48 << 20),
        cost_estimate=pl.CostEstimate(flops=flops, bytes_accessed=size, transcendentals=0),
        name=name,
    )(*arrays)


def swap(array, axis, by):
    count = lax.axis_size(axis)
    return lax.ppermute(array, axis, [(i, i ^ by) for i in range(count)])


def passed(array, axis, by):
    count = lax.axis_size(axis)
    return lax.ppermute(array, axis, [(i, i + by) for i in range(count) if 0 <= i + by < count])


def scan_blocks(pay, forward, out_type):
    count = lax.axis_size("seq")
    place = lax.axis_index("seq")
    ch = pay.shape[1]
    pre = q = None
    by = 1
    while by < count:
        got = swap(pay, "seq", by)
        upper = (place // by) % 2
        flag = jnp.reshape(upper if forward else 1 - upper, (1,)).astype(jnp.int32)
        first, last = by == 1, by * 2 >= count
        outs = [((N, ch), out_type if last else F32)]
        if not last:
            outs += [((8, ch), F32), ((N + TH, ch), BF)]
        args = [flag, pay, got] + ([] if first else [pre, q])
        res = call(
            functools.partial(k_combine, first, last), "combine", args, outs
        )
        pre = res[0]
        if not last:
            q, pay = res[1], res[2]
        by *= 2
    return pre


def to_shares(chunks):
    nh = lax.axis_size("head")
    return [chunks[0]] + [swap(chunks[k], "head", k) for k in range(1, nh)]


def from_shares(share):
    nh = lax.axis_size("head")
    return [share] + [swap(share, "head", k) for k in range(1, nh)]


def layer_forward(layer, src, halo_raw, prm, flags, order, width, cot):
    nh = lax.axis_size("head")
    norm_gain, in_zx, in_bc, in_dt, dtb, alog, skip, cx, cxb, cbc, cbcb, gate_gain, out_proj = prm
    d, ch = in_zx.shape[2], in_zx.shape[3]
    heads = ch // P_SIZE
    t = flags.shape[1]
    cc = ch + 2 * N
    wz, wx = Layered(in_zx, layer, 0), Layered(in_zx, layer, 1)
    wbc, wdt, wo = Layered(in_bc, layer), Layered(in_dt, layer), Layered(out_proj, layer)
    outs = [((t, ch), F32), ((t, cc), BF), ((t, LANES), F32), ((t, d), BF)]
    work = 2 * t * d * (2 * ch + 2 * N + LANES)
    if layer == 0:
        halo = passed(halo_raw, "seq", 1)
        gate, cin, dtr, normed = call(
            functools.partial(k_project, 0, nh), "project0",
            [src, norm_gain, wz, wx, wbc, wdt], outs, flops=work,
        )
        invc = None
    else:
        rows = src[0].shape[0]
        tail = jnp.zeros((HALO, d), BF)
        for k in range(nh):
            tail = jnp.where(order[k] == nh - 1, src[k][rows - HALO :, :d], tail)
        halo = passed(tail, "seq", 1)
        gate, cin, dtr, normed, invc = call(
            functools.partial(k_project, layer, nh), "project1",
            [order, *src, wz, wx, wbc, wdt], outs + [((t, LANES), F32)], flops=work,
        )
    act, ds, hc, step, cum, pay = call(
        functools.partial(k_conv, layer, heads, layer == 0), "conv",
        [halo, norm_gain, cin, dtr, flags, wx, wbc, cx, cxb, cbc, cbcb, dtb, alog],
        [((t, cc), BF), ((t, cc), BF), ((HALO, cc), BF), ((t, LANES), F32), ((t, LANES), F32),
         ((N + TH, ch), BF)],
        [((t + HALO, cc), F32)],
        flops=2 * t * N * ch,
    )
    pre = scan_blocks(pay, True, BF)
    (yin,) = call(
        functools.partial(k_inside, heads), "inside", [act, step, cum, flags], [((t, ch), F32)],
        flops=2 * t * t * ch * 2,
    )
    final = layer == LAYERS - 1
    rows = t // nh
    outs = [((t, ch), F32)] + [((rows, d + LANES), BF)] * nh
    args = [order, pre, act, cum, flags, yin, gate, gate_gain, skip, wo]
    if final:
        args.append(cot)
        outs += [((t, ch), F32), ((8, t), F32)]
    res = call(
        functools.partial(k_output, layer, heads, nh), "output", args, outs,
        [((t, d + LANES), BF)], flops=2 * t * ch * d,
    )
    stored = dict(
        gate=gate, cin=cin, dtr=dtr, normed=normed, act=act, ds=ds, hc=hc, step=step, cum=cum,
        pre=pre, y0=res[0],
    )
    if final:
        stored["gout"], stored["small"] = res[1 + nh], res[2 + nh]
    return res[1 : 1 + nh], invc, stored


def layer_backward(layer, sv, low_src, invc, prm, flags, order, width, own):
    nh = lax.axis_size("head")
    norm_gain, in_zx, in_bc, in_dt, dtb, alog, skip, cx, cxb, cbc, cbcb, gate_gain, out_proj = prm
    d, ch = in_zx.shape[2], in_zx.shape[3]
    heads = ch // P_SIZE
    t = flags.shape[1]
    cc = ch + 2 * N
    rows = t // nh
    wz, wx = Layered(in_zx, layer, 0), Layered(in_zx, layer, 1)
    wbc, wdt, wo = Layered(in_bc, layer), Layered(in_dt, layer), Layered(out_proj, layer)
    outs = [((N + TH, ch), BF), ((t, ch), BF), ((t, ch), BF), ((t, ch), BF), ((8, ch), F32)]
    common = [gate_gain, sv["y0"], sv["gate"], sv["act"], sv["cum"], flags, skip]
    body = functools.partial(k_gate_back, layer, heads, nh)
    if layer == LAYERS - 1:
        pay, gm, lowgate, og, small_g = call(
            body, "gateback1",
            [*from_shares(sv["small"]), sv["gout"], width, *common], outs, flops=2 * t * N * ch,
        )
        low = low_src
    else:
        pay, gm, lowgate, og, small_g, low = call(
            body, "gateback0",
            [order, *low_src, wo, invc, width, *common], outs + [((t, d), BF)],
            [((t, LANES), F32)], flops=2 * t * ch * d,
        )
    state_grad = scan_blocks(pay, False, F32)
    dxs, dbc, w_out, w_z = call(
        functools.partial(k_inside_back, heads), "insideback",
        [sv["act"], sv["step"], sv["cum"], flags, gm, sv["pre"], low, og, sv["normed"], lowgate],
        [((t, ch), F32), ((t, 2 * N), F32), ((ch, d), BF), ((d, ch), BF)],
        flops=2 * t * t * ch * 4 + 4 * t * d * ch,
    )
    gb, gh, lowraw, small = call(
        functools.partial(k_state_back, layer, heads), "stateback",
        [state_grad, sv["pre"], sv["act"], sv["step"], sv["cum"], sv["dtr"], flags, gm, sv["y0"],
         dxs, dbc, sv["ds"], sv["cin"], sv["hc"], cx, cbc, skip, dtb, alog],
        [((t, cc), F32), ((HALO, cc), F32), ((t, LANES), BF), ((8, cc), F32)],
        [((t + HALO, cc), F32), ((t + 2 * HALO, cc), F32)],
        flops=4 * t * N * ch,
    )
    ret = passed(gh, "seq", -1)
    (part,) = call(
        k_back_project, "backproject", [lowgate, gb, lowraw, wz, wx, wbc, wdt], [((t, d), F32)],
        flops=2 * t * d * (2 * ch + 3 * N),
    )
    chunks = call(
        functools.partial(k_back_fix, nh), "backfix", [order, part, ret, wx, wbc],
        [((rows, d), BF)] * nh, [((t, d), BF)], flops=2 * 2 * HALO * d * cc,
    )
    parts = to_shares(chunks)
    w_x, w_bc, w_dt = call(
        k_weights, "weights", [sv["normed"], gb, ret, lowraw],
        [((d, ch), BF), ((d, 2 * N), BF), ((d, LANES), BF)], [((t, cc), BF)],
        flops=2 * t * d * (ch + 3 * N),
    )
    body = functools.partial(k_norm_back, layer, nh)
    if layer > 0:
        r_own, g_in, total = own
        g_own, gng, share = call(
            body, "normback1", [order, *parts, r_own, g_in, norm_gain, total],
            [((rows, d), F32), ((8, d), F32), ((rows, d + LANES), BF)],
        )
    else:
        r_own, g_in = own
        gng, share = call(
            body, "normback0", [order, *parts, r_own, g_in, norm_gain],
            [((8, d), F32), ((rows, d), BF)],
        )
        g_own = None
    grads = dict(
        w_out=w_out, w_z=w_z, w_x=w_x, w_bc=w_bc, w_dt=w_dt, small=small, small_g=small_g,
        gng=gng[0],
    )
    return from_shares(share), g_own, grads


def summed(grads, heads):
    small, small_g = grads["small"], grads["small_g"]
    ch = small_g.shape[1]
    g_skip = jnp.sum(small_g[1].reshape(heads, P_SIZE), axis=1)
    over_seq = [grads["w_z"], grads["w_x"], grads["w_dt"][:, :heads], grads["w_out"]]
    over_seq = [lax.psum(a, "seq").astype(F32) for a in over_seq]
    w_bc = lax.psum(grads["w_bc"], ("seq", "head")).astype(F32)
    flat = lax.psum(
        jnp.concatenate(
            [small[:5, :ch].reshape(-1), small_g[0], g_skip, small[5, :heads], small[6, :heads]]
        ),
        "seq",
    )
    both = lax.psum(
        jnp.concatenate([small[:5, ch:].reshape(-1), grads["gng"]]), ("seq", "head")
    )
    w_z, w_x, w_dt, w_out = over_seq
    x_rows = flat[: 5 * ch].reshape(5, ch)
    rest = flat[5 * ch :]
    bc = both[: 5 * 2 * N].reshape(5, 2 * N)
    return (
        both[5 * 2 * N :],
        jnp.stack([w_z, w_x]),
        w_bc,
        w_dt,
        rest[ch + heads : ch + 2 * heads],
        rest[ch + 2 * heads : ch + 3 * heads],
        rest[ch : ch + heads],
        x_rows[:4],
        x_rows[4],
        bc[:4],
        bc[4],
        rest[:ch],
        w_out,
    )


def per_device(
    stream, seq_flags, norm_gain, in_zx, in_bc, in_dt, dt_bias, a_log, skip_d, conv_x,
    conv_x_bias, conv_bc, conv_bc_bias, gate_gain, out_proj, cotangent,
):
    nh = lax.axis_size("head")
    t, d = stream.shape
    ch = in_zx.shape[3]
    heads = ch // P_SIZE
    rows = t // nh
    pad = LANES - heads
    flags = seq_flags.reshape(1, t)
    dt_pad = jnp.pad(in_dt, ((0, 0), (0, 0), (0, pad)))
    dtb, alog, skip = (jnp.pad(a, ((0, 0), (0, pad))) for a in (dt_bias, a_log, skip_d))
    prm = (
        norm_gain, in_zx, in_bc, dt_pad, dtb, alog, skip, conv_x, conv_x_bias, conv_bc,
        conv_bc_bias, gate_gain, out_proj,
    )
    order = lax.axis_index("head") ^ jnp.arange(nh, dtype=jnp.int32)
    width = jnp.full((1,), 1.0 / (ch * nh), F32)

    chunks, _, sv0 = layer_forward(
        0, stream, stream[t - HALO :], prm, flags, order, width, cotangent
    )
    r1, total0, share = call(
        functools.partial(k_stream, 0, nh), "stream0",
        [order, *to_shares(chunks), stream, norm_gain, width],
        [((rows, d), F32), ((rows, d), F32), ((rows, d + LANES), BF)],
    )
    chunks, invc0, sv1 = layer_forward(
        1, from_shares(share), None, prm, flags, order, width, cotangent
    )
    low, g1, grads1 = layer_backward(
        1, sv1, cotangent, None, prm, flags, order, width, (r1, cotangent, total0)
    )
    (out_share,) = call(
        functools.partial(k_stream_last, nh), "stream1",
        [order, *to_shares(chunks), r1, width], [((rows, d), BF)],
    )
    (output,) = call(
        functools.partial(k_join, nh), "join", [order, *from_shares(out_share)], [((t, d), F32)]
    )
    last, _, grads0 = layer_backward(
        0, sv0, low, invc0, prm, flags, order, width, (stream, g1)
    )
    (grad_stream,) = call(
        functools.partial(k_join, nh), "join", [order, *last], [((t, d), F32)]
    )
    per_layer = [summed(grads0, heads), summed(grads1, heads)]
    stacked = [jnp.stack(pair) for pair in zip(*per_layer)]
    return (output, grad_stream, *stacked)


def solution(mesh):
    placed = (
        P("seq", None),
        P("seq"),
        P(),
        P(None, None, None, "head"),
        P(),
        P(None, None, "head"),
        P(None, "head"),
        P(None, "head"),
        P(None, "head"),
        P(None, None, "head"),
        P(None, "head"),
        P(),
        P(),
        P(None, "head"),
        P(None, "head", None),
        P("seq", None),
    )
    return jax.shard_map(
        per_device,
        mesh=mesh,
        in_specs=placed,
        out_specs=(
            P("seq", None),
            P("seq", None),
            P(),
            P(None, None, None, "head"),
            P(),
            P(None, None, "head"),
            P(None, "head"),
            P(None, "head"),
            P(None, "head"),
            P(None, None, "head"),
            P(None, "head"),
            P(),
            P(),
            P(None, "head"),
            P(None, "head", None),
        ),
        check_vma=False,
    )
```

```python
import functools

import jax
import jax.numpy as jnp
from jax import lax
from jax.experimental import pallas as pl
from jax.experimental.pallas import tpu as pltpu
from jax.sharding import PartitionSpec as P

P_SIZE = 64
N = 128
LAYERS = 2
EPS = 1e-05
LANES = 128
HALO = 8
TH = 16
F32 = jnp.float32
BF = jnp.bfloat16
HI = lax.Precision.HIGHEST


def dot(a, b, dims=((1,), (0,)), precision=None):
    return lax.dot_general(a, b, (dims, ((), ())), preferred_element_type=F32, precision=precision)


NT = ((1,), (1,))
TN = ((0,), (0,))


def iotas(rows, cols):
    return (
        lax.broadcasted_iota(jnp.int32, (rows, cols), 0),
        lax.broadcasted_iota(jnp.int32, (rows, cols), 1),
    )


def tri(rows, lower=True):
    r, c = iotas(rows, rows)
    return jnp.where(c <= r if lower else c >= r, 1.0, 0.0)


def flags8(flags_ref):
    return jnp.broadcast_to(flags_ref[...].astype(F32), (8, flags_ref.shape[1])).astype(BF)


def seg_col(flags_ref):
    t = flags_ref.shape[1]
    return dot(tri(t).astype(BF), flags8(flags_ref), NT)[:, 0:1]


def seg_row(flags_ref):
    t = flags_ref.shape[1]
    return dot(flags8(flags_ref), tri(t, False).astype(BF))[0:1, :]


def windows(flags_ref, taps):
    t = flags_ref.shape[1]
    r, c = iotas(t, t)
    fl = flags8(flags_ref)
    out = [None]
    for d in range(1, taps):
        band = jnp.where((c <= r) & (c > r - d), 1.0, 0.0).astype(BF)
        out.append(jnp.where(dot(band, fl, NT)[:, 0:1] == 0.0, 1.0, 0.0))
    return out


def spread(cols, heads):
    rows = cols.shape[0]
    return jnp.concatenate(
        [jnp.broadcast_to(cols[:, h : h + 1], (rows, P_SIZE)) for h in range(heads)], axis=1
    )


def head_sum(z):
    r, c = iotas(z.shape[1], LANES)
    lo = c * P_SIZE
    pick = jnp.where((r >= lo) & (r < lo + P_SIZE), 1.0, 0.0)
    return dot(z, pick, precision=HI)


def sigmoid(v):
    return 1.0 / (1.0 + jnp.exp(-v))


def softplus(v):
    return jnp.maximum(v, 0.0) + jnp.log(1.0 + jnp.exp(-jnp.abs(v)))


def two(col, width):
    rows = col.shape[0]
    _, c = iotas(rows, width)
    high = col.astype(BF).astype(F32)
    low = col - high
    return jnp.where(c == 0, high, jnp.where(c == 1, low, 0.0)).astype(BF)


def untwo(block):
    b = block.astype(F32)
    return b[:, 0:1] + b[:, 1:2]


def through_rows(row):
    r, _ = iotas(TH, row.shape[1])
    high = row.astype(BF).astype(F32)
    return jnp.where(r == 0, high, jnp.where(r == 1, row - high, 0.0)).astype(BF)


def closing_parts(cum, segc):
    t = cum.shape[0]
    last, seg_last = cum[t - 1 : t, :], segc[t - 1 : t, :]
    closing = jnp.exp(last - cum) * jnp.where(segc == seg_last, 1.0, 0.0)
    through = jnp.exp(last) * jnp.where(seg_last == 0.0, 1.0, 0.0)
    return closing, through


def norm_of(r, gain):
    inv = lax.rsqrt(jnp.mean(r * r, axis=1, keepdims=True) + EPS)
    return r * inv * gain


def at_rows(s_ref, k, rows):
    return pl.ds(pl.multiple_of(s_ref[k] * rows, rows), rows)


def k_project(layer, nh, refs):
    if layer == 0:
        stream, gain, wz, wx, wbc, wdt, gate, cin, dtr, normed = refs
        nm = norm_of(stream[...].astype(F32), gain[0:1, :]).astype(BF)
        normed[...] = nm
    else:
        s_ref, chunks, refs = refs[0], refs[1 : 1 + nh], refs[1 + nh :]
        wz, wx, wbc, wdt, gate, cin, dtr, normed, invc = refs
        rows, d = chunks[0].shape[0], normed.shape[1]
        for k in range(nh):
            normed[at_rows(s_ref, k, rows), :] = chunks[k][:, :d]
            both = jnp.broadcast_to(untwo(chunks[k][:, d:]), (rows, LANES))
            invc[at_rows(s_ref, k, rows), :] = both
        nm = normed[...]
    ch = wz.shape[1]
    gate[...] = dot(nm, wz[...])
    cin[:, :ch] = dot(nm, wx[...]).astype(BF)
    cin[:, ch:] = dot(nm, wbc[...]).astype(BF)
    dtr[...] = dot(nm, wdt[...])


def k_conv(layer, heads, raw_halo, refs):
    (halo, gain, cin, dtr, flags, wx, wbc, cx, cxb, cbc, cbcb, dtb, alog,
     act, ds, hc, step, cum, pay, ext) = refs
    t, cc = cin.shape
    ch = wx.shape[1]
    taps = cx.shape[1]
    hn = halo[...]
    if raw_halo:
        hn = norm_of(hn.astype(F32), gain[layer : layer + 1, :]).astype(BF)
    hx, hb = dot(hn, wx[...]).astype(BF), dot(hn, wbc[...]).astype(BF)
    hc[:, :ch] = hx
    hc[:, ch:] = hb
    ext[:HALO, :ch] = hx.astype(F32)
    ext[:HALO, ch:] = hb.astype(F32)
    ext[HALO:, :] = cin[...].astype(F32)
    valid = windows(flags, taps)
    for lo, hi, w, b in ((0, ch, cx, cxb), (ch, cc, cbc, cbcb)):
        v = b[layer : layer + 1, :] + w[layer, taps - 1 : taps, :] * ext[HALO:, lo:hi]
        for d in range(1, taps):
            tap = w[layer, taps - 1 - d : taps - d, :]
            v = v + tap * (ext[HALO - d : HALO - d + t, lo:hi] * valid[d])
        sig = sigmoid(v)
        act[:, lo:hi] = (v * sig).astype(BF)
        ds[:, lo:hi] = (sig * (1.0 + v * (1.0 - sig))).astype(BF)
    st = softplus(dtr[...] + dtb[layer : layer + 1, :])
    rate = -jnp.exp(alog[layer : layer + 1, :])
    cm = dot(tri(t), st * rate, precision=HI)
    step[...] = st
    cum[...] = cm
    closing, through = closing_parts(cm, seg_col(flags))
    x = act[:, :ch].astype(F32)
    xs = (x * spread(st * closing, heads)).astype(BF)
    pay[:N, :] = dot(act[:, ch : ch + N], xs, TN).astype(BF)
    pay[N:, :] = through_rows(spread(through, heads))


def k_combine(first, last, refs):
    flag, own, got = refs[0], refs[1], refs[2]
    refs = refs[3:]
    if not first:
        pre, q = refs[0], refs[1]
        refs = refs[2:]
    mine = flag[0] == 1
    s_own, s_got = own[:N, :].astype(F32), got[:N, :].astype(F32)
    t_own = own[N : N + 1, :].astype(F32) + own[N + 1 : N + 2, :].astype(F32)
    t_got = got[N : N + 1, :].astype(F32) + got[N + 1 : N + 2, :].astype(F32)
    if first:
        new_pre = jnp.where(mine, s_got, 0.0)
        new_q = jnp.where(mine, t_got, 1.0)
    else:
        qv = q[0:1, :]
        new_pre = pre[...] + jnp.where(mine, qv * s_got, 0.0)
        new_q = qv * jnp.where(mine, t_got, 1.0)
    refs[0][...] = new_pre.astype(refs[0].dtype)
    if not last:
        refs[1][...] = jnp.broadcast_to(new_q, (8, new_q.shape[1]))
        total = refs[2]
        total[:N, :] = (
            jnp.where(mine, s_own, s_got)
            + jnp.where(mine, t_own, t_got) * jnp.where(mine, s_got, s_own)
        ).astype(BF)
        total[N:, :] = through_rows(t_own * t_got)


def decay_of(cum_col, cum_row, allowed):
    return jnp.exp(jnp.where(allowed, cum_col - cum_row, -1e30))


def k_inside(heads, refs):
    act, step, cum, flags, yin = refs
    t = act.shape[0]
    ch = yin.shape[1]
    r, c = iotas(t, t)
    allowed = (c <= r) & (seg_col(flags) == seg_row(flags))
    scores = dot(act[:, ch + N :], act[:, ch : ch + N], NT)
    cm = cum[...]
    cmt = cm.T
    xs = (act[:, :ch].astype(F32) * spread(step[...], heads)).astype(BF)
    for h in range(heads):
        m = decay_of(cm[:, h : h + 1], cmt[h : h + 1, :], allowed) * scores
        cols = slice(h * P_SIZE, (h + 1) * P_SIZE)
        yin[:, cols] = dot(m.astype(BF), xs[:, cols])


def k_output(layer, heads, nh, refs):
    s_ref, pre, act, cum, flags, yin, gate, gain, skip, wo = refs[:10]
    refs = refs[10:]
    final = layer == LAYERS - 1
    if final:
        low = refs[0]
        refs = refs[1:]
    y0, refs = refs[0], refs[1:]
    chunks, refs = refs[:nh], refs[nh:]
    ch = yin.shape[1]
    d = wo.shape[1]
    opening = jnp.exp(cum[...]) * jnp.where(seg_col(flags) == 0.0, 1.0, 0.0)
    y = yin[...] + dot(act[:, ch + N :], pre[...]) * spread(opening, heads)
    y0[...] = y
    mixed = y + spread(skip[layer : layer + 1, :], heads) * act[:, :ch].astype(F32)
    gi = gate[...]
    gated = mixed * (gi * sigmoid(gi))
    sq = jnp.sum(gated * gated, axis=1, keepdims=True)
    scaled = gated * gain[layer : layer + 1, :]
    scratch = refs[-1]
    scratch[:, :d] = dot(scaled.astype(BF), wo[...]).astype(BF)
    scratch[:, d:] = two(sq, LANES)
    rows = chunks[0].shape[0]
    for k in range(nh):
        chunks[k][...] = scratch[at_rows(s_ref, k, rows), :]
    if final:
        gout, small = refs[0], refs[1]
        go = dot(low[...], wo[...], NT)
        gout[...] = go
        cross = jnp.sum(go * scaled, axis=1, keepdims=True)
        t = sq.shape[0]
        _, c = iotas(t, LANES)
        cols = jnp.where(c == 0, sq, jnp.where(c == 1, cross, 0.0))
        small[...] = cols.T[:8, :]


def k_stream(layer, nh, refs):
    s_ref, parts, refs = refs[0], refs[1 : 1 + nh], refs[1 + nh :]
    own, gain, width, r_out, tot_out, pay = refs[:3] + refs[3:]
    rows, wide = parts[0].shape
    d = wide - LANES
    total = parts[0][:, :d].astype(F32)
    sq = untwo(parts[0][:, d:])
    for p in parts[1:]:
        total = total + p[:, :d].astype(F32)
        sq = sq + untwo(p[:, d:])
    inv = lax.rsqrt(sq * width[0] + EPS)
    r = own[at_rows(s_ref, 0, rows), :].astype(F32) + total * inv
    r_out[...] = r
    tot_out[...] = total
    pay[:, :d] = norm_of(r, gain[layer + 1 : layer + 2, :]).astype(BF)
    pay[:, d:] = two(inv, LANES)


def k_stream_last(nh, refs):
    s_ref, parts, refs = refs[0], refs[1 : 1 + nh], refs[1 + nh :]
    own, width, r_out = refs
    rows, wide = parts[0].shape
    d = wide - LANES
    total = parts[0][:, :d].astype(F32)
    sq = untwo(parts[0][:, d:])
    for p in parts[1:]:
        total = total + p[:, :d].astype(F32)
        sq = sq + untwo(p[:, d:])
    r_out[...] = (own[...] + total * lax.rsqrt(sq * width[0] + EPS)).astype(BF)


def k_join(nh, refs):
    s_ref, parts, out = refs[0], refs[1 : 1 + nh], refs[1 + nh]
    rows = parts[0].shape[0]
    for k in range(nh):
        out[at_rows(s_ref, k, rows), :] = parts[k][...].astype(F32)


def k_gate_back(layer, heads, nh, refs):
    final = layer == LAYERS - 1
    if final:
        smalls, refs = refs[:nh], refs[nh:]
        gout, width, gain, y0, gate, act, cum, flags, skip = refs[:9]
        refs = refs[9:]
        acc = smalls[0][...]
        for s in smalls[1:]:
            acc = acc + s[...]
        t = acc.shape[1]
        cols = jnp.concatenate([acc, jnp.zeros((LANES - 8, t), F32)], axis=0).T
        inv = lax.rsqrt(cols[:, 0:1] * width[0] + EPS)
        cross = cols[:, 1:2]
        go = gout[...]
        pay, gm, lowgate, og, small = refs
    else:
        s_ref, chunks, refs = refs[0], refs[1 : 1 + nh], refs[1 + nh :]
        wo, invc, width, gain, y0, gate, act, cum, flags, skip = refs[:10]
        pay, gm, lowgate, og, small, low, crs = refs[10:]
        rows, d = chunks[0].shape[0], wo.shape[1]
        for k in range(nh):
            low[at_rows(s_ref, k, rows), :] = chunks[k][:, :d]
            both = jnp.broadcast_to(untwo(chunks[k][:, d:]), (rows, LANES))
            crs[at_rows(s_ref, k, rows), :] = both
        cross = crs[:, 0:1]
        inv = invc[:, 0:1]
        go = dot(low[...], wo[...], NT)
    ch = y0.shape[1]
    gn = gain[layer : layer + 1, :]
    x = act[:, :ch].astype(F32)
    mixed = y0[...] + spread(skip[layer : layer + 1, :], heads) * x
    gi = gate[...]
    sig = sigmoid(gi)
    silu = gi * sig
    gated = mixed * silu
    ginv = gated * inv
    og[...] = (ginv * gn).astype(BF)
    g_gated = inv * (gn * go) - ginv * (inv * inv * cross * width[0])
    g_mixed = g_gated * silu
    lowgate[...] = (g_gated * mixed * (sig * (1.0 + gi * (1.0 - sig)))).astype(BF)
    gm[...] = g_mixed.astype(BF)
    segc = seg_col(flags)
    cm = cum[...]
    opening = jnp.exp(cm) * jnp.where(segc == 0.0, 1.0, 0.0)
    _, through = closing_parts(cm, segc)
    grad = dot(act[:, ch + N :], (g_mixed * spread(opening, heads)).astype(BF), TN)
    pay[:N, :] = grad.astype(BF)
    pay[N:, :] = through_rows(spread(through, heads))
    r, _ = iotas(8, ch)
    row0 = jnp.sum(go * ginv, axis=0, keepdims=True)
    row1 = jnp.sum(g_mixed * x, axis=0, keepdims=True)
    small[...] = jnp.where(r == 0, row0, jnp.where(r == 1, row1, 0.0))


def k_inside_back(heads, refs):
    act, step, cum, flags, gm, pre, dxs, dbc = refs
    t, ch = gm.shape
    r, c = iotas(t, t)
    segc = seg_col(flags)
    allowed = (c <= r) & (segc == seg_row(flags))
    keys, queries = act[:, ch : ch + N], act[:, ch + N :]
    scores = dot(queries, keys, NT)
    cm = cum[...]
    cmt = cm.T
    xs = (act[:, :ch].astype(F32) * spread(step[...], heads)).astype(BF)
    dy = gm[...]
    acc = jnp.zeros((t, t), F32)
    for h in range(heads):
        cols = slice(h * P_SIZE, (h + 1) * P_SIZE)
        decay = decay_of(cm[:, h : h + 1], cmt[h : h + 1, :], allowed)
        m = (decay * scores).astype(BF)
        dxs[:, cols] = dot(m, dy[:, cols], TN)
        acc = acc + dot(dy[:, cols], xs[:, cols], NT) * decay
    low_s = acc.astype(BF)
    dbc[:, :N] = dot(low_s, queries, TN)
    opening = jnp.exp(cm) * jnp.where(segc == 0.0, 1.0, 0.0)
    carried = (dy.astype(F32) * spread(opening, heads)).astype(BF)
    dbc[:, N:] = dot(low_s, keys) + dot(carried, pre[...], NT)


def k_state_back(layer, heads, refs):
    (g, pre, act, step, cum, dtr, flags, gm, y0, dxs, dbc, ds, cin, hc, cx, cbc, skip, dtb, alog,
     gb, gh, lowraw, small, ext, u_ref) = refs
    t, ch = gm.shape
    cc = cin.shape[1]
    taps = cx.shape[1]
    segc = seg_col(flags)
    cm = cum[...]
    st = step[...]
    closing, through = closing_parts(cm, segc)
    x = act[:, :ch].astype(F32)
    st_ch = spread(st, heads)
    clo_ch = spread(closing, heads)
    xs = (x * st_ch).astype(BF)
    xsf = xs.astype(F32)
    gst = g[...]
    gb16 = gst.astype(BF)
    keys = act[:, ch : ch + N]
    dwc = dot(keys, gb16) * clo_ch
    dkeys = dbc[:, :N] + dot((xsf * clo_ch).astype(BF), gb16, NT)
    dx_all = dxs[...] + dwc
    gmf = gm[...].astype(F32)
    z = head_sum(x * dx_all)
    dcum = head_sum(gmf * y0[...] - xsf * dx_all)
    at_last = jnp.sum(head_sum(xsf * dwc), axis=0, keepdims=True)
    keep = jnp.sum(gst * pre[...].astype(F32), axis=0, keepdims=True)
    at_last = at_last + through * head_sum(jnp.broadcast_to(keep, (8, ch)))[0:1, :]
    ddecay = dot(tri(t, False), dcum, precision=HI) + at_last
    rate = -jnp.exp(alog[layer : layer + 1, :])
    graw = (z + ddecay * rate) * sigmoid(dtr[...] + dtb[layer : layer + 1, :])
    lowraw[...] = graw.astype(BF)
    g_alog = jnp.sum(ddecay * st, axis=0, keepdims=True) * rate
    g_dtb = jnp.sum(graw, axis=0, keepdims=True)
    ext[:HALO, :] = hc[...].astype(F32)
    ext[HALO:, :] = cin[...].astype(F32)
    gv_x = (dx_all * st_ch + spread(skip[layer : layer + 1, :], heads) * gmf)
    valid = windows(flags, taps)
    for lo, hi, w, val in (
        (0, ch, cx, gv_x),
        (ch, ch + N, cbc, dkeys),
        (ch + N, cc, cbc, dbc[:, N:]),
    ):
        wl = lo if lo < ch else lo - ch
        gv = val * ds[:, lo:hi].astype(F32)
        small[4:5, lo:hi] = jnp.sum(gv, axis=0, keepdims=True)
        total = None
        for d in range(taps):
            u = gv if d == 0 else gv * valid[d]
            k = taps - 1 - d
            small[k : k + 1, lo:hi] = jnp.sum(
                u * ext[HALO - d : HALO - d + t, lo:hi], axis=0, keepdims=True
            )
            u_ref[0:HALO, lo:hi] = jnp.zeros((HALO, hi - lo), F32)
            u_ref[HALO : HALO + t, lo:hi] = u
            u_ref[HALO + t :, lo:hi] = jnp.zeros((HALO, hi - lo), F32)
            term = w[layer, k : k + 1, wl : wl + hi - lo] * u_ref[d : d + t + HALO, lo:hi]
            total = term if total is None else total + term
        gh[:, lo:hi] = total[:HALO, :]
        gb[:, lo:hi] = total[HALO:, :]
    small[5:8, :] = jnp.zeros((3, cc), F32)
    small[5:6, :LANES] = g_dtb
    small[6:7, :LANES] = g_alog


def k_back_project(refs):
    lowgate, gb, lowraw, wz, wx, wbc, wdt, part = refs
    ch = wz.shape[1]
    part[...] = (
        dot(lowgate[...], wz[...], NT)
        + dot(gb[:, :ch].astype(BF), wx[...], NT)
        + dot(gb[:, ch:].astype(BF), wbc[...], NT)
        + dot(lowraw[...], wdt[...], NT)
    )


def k_back_fix(layer, nh, refs):
    s_ref, part, ret, wx, wbc, normed, gain = refs[:7]
    chunks, gng, scratch = refs[7 : 7 + nh], refs[7 + nh], refs[8 + nh]
    t = part.shape[0]
    ch = wx.shape[1]
    scratch[...] = part[...].astype(BF)
    low = ret[...].astype(BF)
    fix = dot(low[:, :ch], wx[...], NT) + dot(low[:, ch:], wbc[...], NT)
    fix = jnp.concatenate([jnp.zeros_like(fix), fix], axis=0)
    scratch[t - 2 * HALO :, :] = (part[t - 2 * HALO :, :] + fix).astype(BF)
    rows = chunks[0].shape[0]
    for k in range(nh):
        chunks[k][...] = scratch[at_rows(s_ref, k, rows), :]
    products = jnp.sum(scratch[...].astype(F32) * normed[...].astype(F32), axis=0, keepdims=True)
    r, _ = iotas(8, products.shape[1])
    gng[...] = jnp.where(r == 0, products / gain[layer : layer + 1, :], 0.0)


def k_grads(refs):
    (s_ref, normed, gb, ret, lowraw, small, small_g, gng, lowgate, low_g, og,
     keep, send, pack, low) = refs
    nm = normed[...]
    t, cc = gb.shape
    ch = cc - 2 * N
    d = nm.shape[1]
    low[...] = gb[...].astype(BF)
    fix = jnp.concatenate([jnp.zeros_like(ret[...]), ret[...]], axis=0)
    low[t - 2 * HALO :, :] = (gb[t - 2 * HALO :, :] + fix).astype(BF)
    pack[:, :cc] = dot(nm, low[...], TN)
    pack[:, cc : cc + LANES] = dot(nm, lowraw[...], TN)
    rows = jnp.concatenate(
        [
            jnp.zeros((64, cc), F32),
            small[...],
            jnp.concatenate([small_g[...], jnp.zeros((8, cc - ch), F32)], axis=1),
            jnp.zeros((48, cc), F32),
        ],
        axis=0,
    )
    pack[:cc, cc : cc + LANES] = pack[:cc, cc : cc + LANES] + rows.T
    rows = jnp.concatenate([jnp.zeros((80, d), F32), gng[...], jnp.zeros((40, d), F32)], axis=0)
    pack[:, cc : cc + LANES] = pack[:, cc : cc + LANES] + rows.T
    at = cc + LANES
    pack[:, at : at + ch] = dot(nm, lowgate[...], TN)
    pack[:, at + ch : at + 2 * ch] = dot(low_g[...], og[...], TN)
    half = keep.shape[0]
    keep[...] = pack[at_rows(s_ref, 0, half), :].astype(BF)
    send[...] = pack[at_rows(s_ref, 1, half), :].astype(BF)


def k_split(chips, refs):
    s_ref, keep, got = refs[:3]
    chunks, scratch = refs[3 : 3 + chips], refs[3 + chips]
    scratch[...] = keep[...].astype(F32) + got[...].astype(F32)
    rows = chunks[0].shape[0]
    for k in range(chips):
        chunks[k][...] = scratch[at_rows(s_ref, k, rows), :].astype(BF)


def k_sum(chips, ch, refs):
    parts, refs = refs[:chips], refs[chips:]
    total = parts[0][...].astype(F32)
    for p in parts[1:]:
        total = total + p[...].astype(F32)
    refs[0][...] = total.astype(BF)
    if len(refs) > 1:
        refs[1][...] = total[:, ch : ch + 2 * N + LANES].astype(BF)


def k_head_part(nh, ch, refs):
    share, parts, out = refs[0], refs[1 : 1 + nh], refs[1 + nh]
    total = parts[0][...].astype(F32)
    for p in parts[1:]:
        total = total + p[...].astype(F32)
    out[...] = share[...]
    out[:, ch : ch + 2 * N] = total[:, : 2 * N].astype(BF)
    own = share[:, ch + 2 * N : ch + 2 * N + LANES].astype(F32)
    moved = pltpu.roll(total[:, 2 * N :], 32, axis=1)
    _, c = iotas(own.shape[0], LANES)
    out[:, ch + 2 * N : ch + 2 * N + LANES] = jnp.where(c >= 96, moved, own).astype(BF)


def k_finish(chips, last, refs):
    s_ref, mine, theirs, refs = refs[0], refs[1], refs[2], refs[3:]
    if last:
        other, refs = refs[3], refs[4:]
    wzx, wbc, wo, small = refs[:4]
    pack = refs[-1]
    rows = mine.shape[0] // chips
    for k in range(chips):
        for half, src in ((0, mine), (1, theirs)):
            pack[at_rows(s_ref, half * chips + k, rows), :] = src[
                k * rows : (k + 1) * rows, :
            ].astype(F32)
    ch = wzx.shape[-1]
    cc = ch + 2 * N
    at = cc + LANES
    wzx[1] = pack[:, :ch]
    wbc[...] = pack[:, ch:cc]
    small[...] = pack[:, cc:at].T
    wzx[0] = pack[:, at : at + ch]
    wo[...] = pack[:, at + ch : at + 2 * ch].T
    if last:
        gg, dt, cx, cxb, cbc, cbcb, gate, skip, dtb, alog = refs[4:-1]
        heads = dtb.shape[1]
        for l, src in ((0, small), (1, other)):
            gg[l : l + 1, :] = src[112:113, :]
            dt[:, l, :] = src[0:heads, :]
            cx[l] = src[64:68, :ch]
            cxb[l : l + 1, :] = src[68:69, :ch]
            cbc[l] = src[96:100, ch:cc]
            cbcb[l : l + 1, :] = src[100:101, ch:cc]
            gate[l : l + 1, :] = src[72:73, :ch]
            skips = head_sum(jnp.broadcast_to(src[73:74, :ch], (8, ch)))
            skip[l : l + 1, :] = skips[0:1, :heads]
            dtb[l : l + 1, :] = src[69:70, :heads]
            alog[l : l + 1, :] = src[70:71, :heads]


def k_norm_back(layer, nh, refs):
    s_ref, parts, refs = refs[0], refs[1 : 1 + nh], refs[1 + nh :]
    final = layer == LAYERS - 1
    if layer > 0:
        r_own, g_in, gain, total, g_out, pay = refs
    else:
        r_own, g_in, gain, pay = refs
    rows, d = parts[0].shape
    gn = parts[0][...].astype(F32)
    for p in parts[1:]:
        gn = gn + p[...].astype(F32)
    r = r_own[...] if layer > 0 else r_own[at_rows(s_ref, 0, rows), :].astype(F32)
    old = g_in[at_rows(s_ref, 0, rows), :].astype(F32) if final else g_in[...]
    inv = lax.rsqrt(jnp.mean(r * r, axis=1, keepdims=True) + EPS)
    ri = r * inv
    gg = gn * gain[layer : layer + 1, :]
    new = old + inv * (gg - ri * jnp.mean(gg * ri, axis=1, keepdims=True))
    if layer > 0:
        g_out[...] = new
        low = new.astype(BF)
        pay[:, :d] = low
        cross = jnp.sum(low.astype(F32) * total[...], axis=1, keepdims=True)
        pay[:, d:] = two(cross, LANES)
    else:
        pay[...] = new.astype(BF)


SMEM = pl.BlockSpec(memory_space=pltpu.SMEM)


class Layered:
    def __init__(self, array, *lead):
        self.array, self.lead = array, lead


class Whole:
    def __init__(self, array):
        self.array = array


class After(Whole):
    pass


class Part:
    def __init__(self, shape, dtype, *lead):
        self.shape, self.dtype, self.lead = shape, dtype, lead


class Loose:
    def __init__(self, array):
        self.array = array


def call(body, name, args, outs, scratch=(), flops=0, loose=False, aliases=None, after=()):
    count_in = len(args)
    args = list(args) + [After(a) for a in after]
    specs, arrays = [], []
    size = 0
    for a in args:
        if isinstance(a, After):
            specs.append(pl.BlockSpec(memory_space=pltpu.HBM))
            arrays.append(pltpu.with_memory_space_constraint(a.array, pltpu.HBM))
        elif isinstance(a, Whole):
            specs.append(pl.BlockSpec(memory_space=pltpu.HBM))
            arrays.append(a.array)
        elif isinstance(a, Loose):
            a = a.array
            specs.append(pl.BlockSpec(a.shape, functools.partial(lambda n, i: (0,) * n, a.ndim)))
            arrays.append(a)
            size += a.size * a.dtype.itemsize
        elif isinstance(a, Layered):
            rest = a.array.shape[len(a.lead) :]
            lead = a.lead
            specs.append(
                pl.BlockSpec(
                    (None,) * len(lead) + rest,
                    functools.partial(lambda lead, n, i: lead + (0,) * n, lead, len(rest)),
                )
            )
            arrays.append(pltpu.with_memory_space_constraint(a.array, pltpu.HBM))
            count = 1
            for s in rest:
                count *= s
            size += count * a.array.dtype.itemsize
        elif a.dtype == jnp.int32 and a.ndim == 1 or a.ndim == 1:
            specs.append(SMEM)
            arrays.append(a)
        else:
            specs.append(pl.BlockSpec(a.shape, functools.partial(lambda n, i: (0,) * n, a.ndim)))
            arrays.append(pltpu.with_memory_space_constraint(a, pltpu.HBM))
            size += a.size * a.dtype.itemsize
    out_specs, out_shapes = [], []
    for o in outs:
        if isinstance(o, Part):
            rest = o.shape[len(o.lead) :]
            out_specs.append(
                pl.BlockSpec(
                    (None,) * len(o.lead) + rest,
                    functools.partial(lambda lead, n, i: lead + (0,) * n, o.lead, len(rest)),
                )
            )
            shape, dtype = o.shape, o.dtype
            out_shapes.append(pltpu.HBM(shape, dtype))
        else:
            shape, dtype = o[0], o[1]
            rest = shape
            out_specs.append(
                pl.BlockSpec(shape, functools.partial(lambda n, i: (0,) * n, len(shape)))
            )
            free = loose or len(o) > 2
            out_shapes.append(
                jax.ShapeDtypeStruct(shape, dtype) if free else pltpu.HBM(shape, dtype)
            )
        count = 1
        for k in rest:
            count *= k
        size += count * jnp.dtype(dtype).itemsize

    def kernel(*refs):
        body(refs[:count_in] + refs[count_in + len(after) :])

    return pl.pallas_call(
        kernel,
        out_shape=out_shapes,
        grid=(1,),
        in_specs=specs,
        out_specs=out_specs,
        scratch_shapes=[pltpu.VMEM(s, t) for s, t in scratch],
        input_output_aliases=aliases or {},
        compiler_params=pltpu.CompilerParams(vmem_limit_bytes=48 << 20),
        cost_estimate=pl.CostEstimate(flops=flops, bytes_accessed=size, transcendentals=0),
        name=name,
    )(*arrays)


def swap(array, axis, by):
    count = lax.axis_size(axis)
    return lax.ppermute(array, axis, [(i, i ^ by) for i in range(count)])


def passed(array, axis, by):
    count = lax.axis_size(axis)
    return lax.ppermute(array, axis, [(i, i + by) for i in range(count) if 0 <= i + by < count])


def scan_blocks(pay, forward, out_type):
    count = lax.axis_size("seq")
    place = lax.axis_index("seq")
    ch = pay.shape[1]
    pre = q = None
    by = 1
    while by < count:
        got = swap(pay, "seq", by)
        upper = (place // by) % 2
        flag = jnp.reshape(upper if forward else 1 - upper, (1,)).astype(jnp.int32)
        first, last = by == 1, by * 2 >= count
        outs = [((N, ch), out_type if last else F32)]
        if not last:
            outs += [((8, ch), F32), ((N + TH, ch), BF)]
        args = [flag, Loose(pay), Loose(got)] + ([] if first else [Loose(pre), Loose(q)])
        res = call(
            functools.partial(k_combine, first, last), "combine", args, outs, loose=True
        )
        pre = res[0]
        if not last:
            q, pay = res[1], res[2]
        by *= 2
    return pre


def to_shares(chunks):
    nh = lax.axis_size("head")
    return [Loose(chunks[0])] + [Loose(swap(chunks[k], "head", k)) for k in range(1, nh)]


def from_shares(share):
    nh = lax.axis_size("head")
    return [Loose(share)] + [Loose(swap(share, "head", k)) for k in range(1, nh)]


def layer_forward(layer, src, halo_raw, prm, flags, order, width, cot):
    nh = lax.axis_size("head")
    norm_gain, in_zx, in_bc, in_dt, dtb, alog, skip, cx, cxb, cbc, cbcb, gate_gain, out_proj = prm
    d, ch = in_zx.shape[2], in_zx.shape[3]
    heads = ch // P_SIZE
    t = flags.shape[1]
    cc = ch + 2 * N
    wz, wx = Layered(in_zx, layer, 0), Layered(in_zx, layer, 1)
    wbc, wdt, wo = Layered(in_bc, layer), Layered(in_dt, layer), Layered(out_proj, layer)
    outs = [((t, ch), F32), ((t, cc), BF), ((t, LANES), F32), ((t, d), BF)]
    work = 2 * t * d * (2 * ch + 2 * N + LANES)
    if layer == 0:
        halo = passed(halo_raw, "seq", 1)
        gate, cin, dtr, normed = call(
            functools.partial(k_project, 0, nh), "project0",
            [src, norm_gain, wz, wx, wbc, wdt], outs, flops=work,
        )
        invc = None
    else:
        rows = src[0].array.shape[0]
        tail = jnp.zeros((HALO, d), BF)
        for k in range(nh):
            tail = jnp.where(order[k] == nh - 1, src[k].array[rows - HALO :, :d], tail)
        halo = passed(tail, "seq", 1)
        gate, cin, dtr, normed, invc = call(
            functools.partial(k_project, layer, nh), "project1",
            [order, *src, wz, wx, wbc, wdt], outs + [((t, LANES), F32)], flops=work,
        )
    act, ds, hc, step, cum, pay = call(
        functools.partial(k_conv, layer, heads, layer == 0), "conv",
        [Loose(halo), norm_gain, cin, dtr, flags, wx, wbc, cx, cxb, cbc, cbcb, dtb, alog],
        [((t, cc), BF), ((t, cc), BF), ((HALO, cc), BF), ((t, LANES), F32), ((t, LANES), F32),
         ((N + TH, ch), BF, 1)],
        [((t + HALO, cc), F32)],
        flops=2 * t * N * ch,
    )
    pre = scan_blocks(pay, True, BF)
    (yin,) = call(
        functools.partial(k_inside, heads), "inside", [act, step, cum, flags], [((t, ch), F32)],
        flops=2 * t * t * ch * 2,
    )
    final = layer == LAYERS - 1
    rows = t // nh
    outs = [((t, ch), F32)] + [((rows, d + LANES), BF, 1)] * nh
    args = [order, Loose(pre), act, cum, flags, yin, gate, gate_gain, skip, wo]
    if final:
        args.append(cot)
        outs += [((t, ch), F32), ((8, t), F32, 1)]
    res = call(
        functools.partial(k_output, layer, heads, nh), "output", args, outs,
        [((t, d + LANES), BF)], flops=2 * t * ch * d,
    )
    stored = dict(
        gate=gate, cin=cin, dtr=dtr, normed=normed, act=act, ds=ds, hc=hc, step=step, cum=cum,
        pre=pre, y0=res[0],
    )
    if final:
        stored["gout"], stored["small"] = res[1 + nh], res[2 + nh]
    return res[1 : 1 + nh], invc, stored


def layer_backward(layer, sv, low_src, invc, prm, flags, order, width, own, before):
    nh = lax.axis_size("head")
    norm_gain, in_zx, in_bc, in_dt, dtb, alog, skip, cx, cxb, cbc, cbcb, gate_gain, out_proj = prm
    d, ch = in_zx.shape[2], in_zx.shape[3]
    heads = ch // P_SIZE
    t = flags.shape[1]
    cc = ch + 2 * N
    rows = t // nh
    wz, wx = Layered(in_zx, layer, 0), Layered(in_zx, layer, 1)
    wbc, wdt, wo = Layered(in_bc, layer), Layered(in_dt, layer), Layered(out_proj, layer)
    outs = [((N + TH, ch), BF, 1), ((t, ch), BF), ((t, ch), BF), ((t, ch), BF), ((8, ch), F32)]
    common = [gate_gain, sv["y0"], sv["gate"], sv["act"], sv["cum"], flags, skip]
    body = functools.partial(k_gate_back, layer, heads, nh)
    if layer == LAYERS - 1:
        pay, gm, lowgate, og, small_g = call(
            body, "gateback1",
            [*from_shares(sv["small"]), sv["gout"], width, *common], outs, flops=2 * t * N * ch,
        )
        low = low_src
    else:
        pay, gm, lowgate, og, small_g, low = call(
            body, "gateback0",
            [order, *low_src, wo, invc, width, *common], outs + [((t, d), BF)],
            [((t, LANES), F32)], flops=2 * t * ch * d, after=before["gate"],
        )
    state_grad = scan_blocks(pay, False, F32)
    dxs, dbc = call(
        functools.partial(k_inside_back, heads), "insideback",
        [sv["act"], sv["step"], sv["cum"], flags, gm, sv["pre"]],
        [((t, ch), F32), ((t, 2 * N), F32)],
        flops=2 * t * t * ch * 4, after=before["inside"],
    )
    gb, gh, lowraw, small = call(
        functools.partial(k_state_back, layer, heads), "stateback",
        [Loose(state_grad), sv["pre"], sv["act"], sv["step"], sv["cum"], sv["dtr"], flags, gm, sv["y0"],
         dxs, dbc, sv["ds"], sv["cin"], sv["hc"], cx, cbc, skip, dtb, alog],
        [((t, cc), F32), ((HALO, cc), F32, 1), ((t, LANES), BF), ((8, cc), F32)],
        [((t + HALO, cc), F32), ((t + 2 * HALO, cc), F32)],
        flops=4 * t * N * ch, after=before["state"],
    )
    ret = passed(gh, "seq", -1)
    (part,) = call(
        k_back_project, "backproject", [lowgate, gb, lowraw, wz, wx, wbc, wdt], [((t, d), F32)],
        flops=2 * t * d * (2 * ch + 3 * N), after=before["project"],
    )
    *chunks, gng = call(
        functools.partial(k_back_fix, layer, nh), "backfix",
        [order, part, Loose(ret), wx, wbc, sv["normed"], norm_gain],
        [((rows, d), BF, 1)] * nh + [((8, d), F32)], [((t, d), BF)], flops=2 * 2 * HALO * d * cc,
        after=before["fix"],
    )
    parts = to_shares(chunks)
    body = functools.partial(k_norm_back, layer, nh)
    if layer > 0:
        r_own, g_in, total = own
        g_own, share = call(
            body, "normback1", [order, *parts, r_own, g_in, norm_gain, total],
            [((rows, d), F32), ((rows, d + LANES), BF, 1)],
        )
    else:
        r_own, g_in = own
        (share,) = call(
            body, "normback0", [order, *parts, r_own, g_in, norm_gain], [((rows, d), BF)],
        )
        g_own = None
    late = [sv["normed"], gb, Loose(ret), lowraw, small, small_g, gng, lowgate, low, og]
    return from_shares(share), g_own, late, dict(inside=dxs, fix=gng, share=share)


def reduced(grads, ch, before):
    count, nh = lax.axis_size("seq"), lax.axis_size("head")
    chips = count // 2
    place = lax.axis_index("seq")
    core, chip = place % 2, place // 2
    sides = jnp.stack([core, 1 - core]).astype(jnp.int32)
    near = (chip ^ jnp.arange(chips, dtype=jnp.int32)).astype(jnp.int32)
    t, d = grads[0].shape
    wide = 3 * ch + 2 * N + LANES
    half, rows = d // 2, d // count
    keep, send = call(
        k_grads, "grads", [sides, *grads], [((half, wide), BF)] * 2,
        [((d, wide), F32), ((t, ch + 2 * N), BF)], flops=2 * t * d * wide, after=before["grads"],
    )
    got = swap(send, "seq", 1)
    chunks = call(
        functools.partial(k_split, chips), "split", [near, keep, Loose(got)],
        [((rows, wide), BF)] * chips, [((half, wide), F32)],
    )
    parts = [chunks[0]] + [Loose(swap(chunks[k], "seq", 2 * k)) for k in range(1, chips)]
    summed, heads_part = call(
        functools.partial(k_sum, chips, ch), "sum", parts,
        [((rows, wide), BF), ((rows, 2 * N + LANES), BF, 1)], after=before["sum"],
    )
    (share,) = call(
        functools.partial(k_head_part, nh, ch), "headpart", [summed, *from_shares(heads_part)],
        [((rows, wide), BF)], after=before["head"],
    )
    mine = jnp.concatenate([share] + [swap(share, "seq", 2 * k) for k in range(1, chips)], axis=0)
    theirs = swap(mine, "seq", 1)
    order = jnp.concatenate([core * chips + near, (1 - core) * chips + near]).astype(jnp.int32)
    return [order, Loose(mine), Loose(theirs)], dict(split=chunks[0], sum=summed, head=share)


def per_device(
    stream, seq_flags, norm_gain, in_zx, in_bc, in_dt, dt_bias, a_log, skip_d, conv_x,
    conv_x_bias, conv_bc, conv_bc_bias, gate_gain, out_proj, cotangent,
):
    nh = lax.axis_size("head")
    t, d = stream.shape
    ch = in_zx.shape[3]
    heads = ch // P_SIZE
    rows = t // nh
    pad = LANES - heads
    flags = seq_flags.reshape(1, t)
    dt_pad = jnp.pad(in_dt, ((0, 0), (0, 0), (0, pad)))
    dtb, alog, skip = (jnp.pad(a, ((0, 0), (0, pad))) for a in (dt_bias, a_log, skip_d))
    prm = (
        norm_gain, in_zx, in_bc, dt_pad, dtb, alog, skip, conv_x, conv_x_bias, conv_bc,
        conv_bc_bias, gate_gain, out_proj,
    )
    order = lax.axis_index("head") ^ jnp.arange(nh, dtype=jnp.int32)
    width = jnp.full((1,), 1.0 / (ch * nh), F32)

    chunks, _, sv0 = layer_forward(
        0, stream, stream[t - HALO :], prm, flags, order, width, cotangent
    )
    r1, total0, share = call(
        functools.partial(k_stream, 0, nh), "stream0",
        [order, *to_shares(chunks), stream, norm_gain, width],
        [((rows, d), F32), ((rows, d), F32), ((rows, d + LANES), BF, 1)],
    )
    chunks, invc0, sv1 = layer_forward(
        1, from_shares(share), None, prm, flags, order, width, cotangent
    )
    none = dict(gate=[], inside=[], state=[], project=[], fix=[])
    low, g1, grads1, _ = layer_backward(
        1, sv1, cotangent, None, prm, flags, order, width, (r1, cotangent, total0), none
    )
    held = dict(grads=[], sum=[], head=[])
    pieces1, marks = reduced(grads1, ch, held)
    before = dict(none, gate=[marks["split"]], inside=[marks["sum"]])
    last, _, grads0, done = layer_backward(
        0, sv0, low, invc0, prm, flags, order, width, (stream, g1), before
    )
    (grad_stream,) = call(
        functools.partial(k_join, nh), "join", [order, *last], [((t, d), F32)]
    )
    pieces0, marks = reduced(grads0, ch, dict(grads=[], sum=[done["share"]], head=[]))
    (out_share,) = call(
        functools.partial(k_stream_last, nh), "stream1",
        [order, *to_shares(chunks), r1, width], [((rows, d), BF, 1)],
    )
    (output,) = call(
        functools.partial(k_join, nh), "join", [order, *from_shares(out_share)], [((t, d), F32)]
    )
    chips = lax.axis_size("seq") // 2
    wide = 3 * ch + 2 * N + LANES
    scratch = [((d, wide), F32)]

    def outs(layer):
        return [
            Part(in_zx.shape, F32, layer), Part(in_bc.shape, F32, layer),
            Part(out_proj.shape, F32, layer), ((LANES, d), F32),
        ]

    g_zx, g_bc, g_wo, small1 = call(
        functools.partial(k_finish, chips, False), "finish1", pieces1, outs(1), scratch
    )
    tiny = [
        (LAYERS, d), (heads, LAYERS, d), conv_x.shape, conv_x_bias.shape, conv_bc.shape,
        conv_bc_bias.shape, gate_gain.shape, skip_d.shape, dt_bias.shape, a_log.shape,
    ]
    g_zx, g_bc, g_wo, _, gg, g_dt, cx, cxb, cbc, cbcb, gate, g_skip, g_dtb, g_alog = call(
        functools.partial(k_finish, chips, True), "finish0",
        [*pieces0, Whole(g_zx), Whole(g_bc), Whole(g_wo), small1],
        outs(0) + [(shape, F32) for shape in tiny], scratch, aliases={3: 0, 4: 1, 5: 2},
    )
    return (
        output, grad_stream, gg, g_zx, g_bc, jnp.transpose(g_dt, (1, 2, 0)), g_dtb, g_alog,
        g_skip, cx, cxb, cbc, cbcb, gate, g_wo,
    )


def solution(mesh):
    placed = (
        P("seq", None),
        P("seq"),
        P(),
        P(None, None, None, "head"),
        P(),
        P(None, None, "head"),
        P(None, "head"),
        P(None, "head"),
        P(None, "head"),
        P(None, None, "head"),
        P(None, "head"),
        P(),
        P(),
        P(None, "head"),
        P(None, "head", None),
        P("seq", None),
    )
    return jax.shard_map(
        per_device,
        mesh=mesh,
        in_specs=placed,
        out_specs=(
            P("seq", None),
            P("seq", None),
            P(),
            P(None, None, None, "head"),
            P(),
            P(None, None, "head"),
            P(None, "head"),
            P(None, "head"),
            P(None, "head"),
            P(None, None, "head"),
            P(None, "head"),
            P(),
            P(),
            P(None, "head"),
            P(None, "head", None),
        ),
        check_vma=False,
    )
```
